256 devices in a mesh: gx: 16 (over z_lo, x), gy: 16 (over y, z_hi, core).
Axes of the slice: x: 4, y: 4, z: 8 (z_hi: 2, z_lo: 4; z = z_hi * 4 + z_lo), core: 2. Of those that a mesh axis runs over, the one named last changes fastest.
Arguments:
- features: float32 [16, 128, 256, 128], P(None, 'gx', 'gy'), may hold values from -6 to 6
- conv_weight: float32 [27, 16, 16], replicated, may hold values from -0.3125 to 0.3125
- mix_weight: float32 [2, 16, 16, 16, 432], P(None, None, None, 'gy', 'gx'), may hold values from -1 to 1
Outputs:
- layer_out: float32 [16, 128, 256, 128], P(None, 'gx', 'gy')
The draws below stay inside these ranges and needn't reach their ends.
All inputs are finite; a program needn't handle non-finite values.
Results may differ from the reference program's by a relative error of at most 0.0001.
Values sent between devices are 32-bit elements; how exact they have to be, the bound alone decides.
A program may use at most 128 MiB of HBM per device.

```python
import math
import jax
import jax.numpy as jnp
from jax import lax

C = 16
NZ = 128
KX = 24
KY = 24
KZ = 12
NX = 128
NY = 256
KYZ_DEV = 18
N_GY = 16


def shard_levels(key, dims, pieces, low, high):
    level = 1.0
    for axis_at, shards_of in pieces:
        draws = jax.random.uniform(jax.random.fold_in(jax.random.fold_in(key, 6), axis_at), (shards_of,), jnp.float32, low / len(pieces), high / len(pieces))
        level = level * jnp.repeat(jnp.exp(draws), dims[axis_at] // shards_of).reshape((-1,) + (1,) * (len(dims) - 1 - axis_at))
    return level


def normal_values(key, dims, deviation, limit, cuts=(), kind=jnp.bfloat16):
    array = jax.random.normal(key, dims, jnp.float32) * deviation
    if len(cuts) > 0:
        array = shard_levels(key, dims, cuts, -0.22, 0.18) * array
    return jnp.clip(array, min=-limit, max=limit).astype(kind)


def setup_inputs(seed: int = 0) -> dict:
    keys = jax.random.split(jax.random.key(seed), 4)
    features = normal_values(keys[0], (C, NX, NY, NZ), 1.0, 6.0, ((1, 16), (2, 16)), jnp.float32)
    conv_weight = normal_values(keys[1], (27, C, C), (27 * C) ** -0.5, 0.3125, (), jnp.float32)
    mix_weight = normal_values(keys[2], (2, C, C, N_GY, KX * KYZ_DEV), 0.177, 1.0, ((3, 16), (4, 16)), jnp.float32)
    return dict(features=features, conv_weight=conv_weight, mix_weight=mix_weight)


PRECISE = lax.Precision.HIGHEST

def angle_tables(positions, frequencies, length):
    product = positions[:, None] * frequencies[None, :] % length
    angles = product.astype(jnp.float32) * (2.0 * math.pi / length)
    return (jnp.cos(angles), jnp.sin(angles))

def kept_frequencies(amount, length):
    index = jnp.arange(amount, dtype=jnp.int32)
    return jnp.where(index < amount // 2, index, length - amount + index).astype(jnp.int32)

def reference(features, conv_weight, mix_weight):
    conv_sum = jnp.zeros(features.shape, jnp.float32)
    for shift_x in (-1, 0, 1):
        for shift_y in (-1, 0, 1):
            for shift_z in (-1, 0, 1):
                offset = 9 * (shift_x + 1) + 3 * (shift_y + 1) + (shift_z + 1)
                moved = jnp.roll(features, (-shift_x, -shift_y, -shift_z), axis=(1, 2, 3))
                conv_sum = conv_sum + jnp.einsum('oi,ixyz->oxyz', conv_weight[offset], moved, precision=PRECISE)
    length_x = features.shape[1]
    length_y = features.shape[2]
    length_z = features.shape[3]
    cos_z, sin_z = angle_tables(jnp.arange(length_z, dtype=jnp.int32), jnp.arange(KZ, dtype=jnp.int32), length_z)
    cos_y, sin_y = angle_tables(jnp.arange(length_y, dtype=jnp.int32), kept_frequencies(KY, length_y), length_y)
    cos_x, sin_x = angle_tables(jnp.arange(length_x, dtype=jnp.int32), kept_frequencies(KX, length_x), length_x)
    z_real = jnp.dot(features, cos_z, precision=PRECISE)
    z_imag = -jnp.dot(features, sin_z, precision=PRECISE)
    y_real = jnp.einsum('cxyk,yq->cxqk', z_real, cos_y, precision=PRECISE) + jnp.einsum('cxyk,yq->cxqk', z_imag, sin_y, precision=PRECISE)
    y_imag = jnp.einsum('cxyk,yq->cxqk', z_imag, cos_y, precision=PRECISE) - jnp.einsum('cxyk,yq->cxqk', z_real, sin_y, precision=PRECISE)
    forward_scale = 1.0 / math.sqrt(length_x * length_y * length_z)
    coef_real = (jnp.einsum('cxqk,xp->cpqk', y_real, cos_x, precision=PRECISE) + jnp.einsum('cxqk,xp->cpqk', y_imag, sin_x, precision=PRECISE)) * forward_scale
    coef_imag = (jnp.einsum('cxqk,xp->cpqk', y_imag, cos_x, precision=PRECISE) - jnp.einsum('cxqk,xp->cpqk', y_real, sin_x, precision=PRECISE)) * forward_scale
    channels = features.shape[0]
    weights = mix_weight.reshape(2, channels, channels, N_GY, KX, KY * KZ // N_GY)
    weights = weights.transpose(0, 1, 2, 4, 3, 5).reshape(2, channels, channels, KX, KY, KZ)
    weight_real = weights[0]
    weight_imag = weights[1]
    mixed_real = jnp.einsum('oipqk,ipqk->opqk', weight_real, coef_real, precision=PRECISE) - jnp.einsum('oipqk,ipqk->opqk', weight_imag, coef_imag, precision=PRECISE)
    mixed_imag = jnp.einsum('oipqk,ipqk->opqk', weight_real, coef_imag, precision=PRECISE) + jnp.einsum('oipqk,ipqk->opqk', weight_imag, coef_real, precision=PRECISE)
    back_real = jnp.einsum('cpqk,xp->cxqk', mixed_real, cos_x, precision=PRECISE) - jnp.einsum('cpqk,xp->cxqk', mixed_imag, sin_x, precision=PRECISE)
    back_imag = jnp.einsum('cpqk,xp->cxqk', mixed_imag, cos_x, precision=PRECISE) + jnp.einsum('cpqk,xp->cxqk', mixed_real, sin_x, precision=PRECISE)
    plane_real = jnp.einsum('cxqk,yq->cxyk', back_real, cos_y, precision=PRECISE) - jnp.einsum('cxqk,yq->cxyk', back_imag, sin_y, precision=PRECISE)
    plane_imag = jnp.einsum('cxqk,yq->cxyk', back_imag, cos_y, precision=PRECISE) + jnp.einsum('cxqk,yq->cxyk', back_real, sin_y, precision=PRECISE)
    inverse_scale = 1.0 / math.sqrt(KX * KY * KZ)
    spectral = (jnp.dot(plane_real, cos_z.T, precision=PRECISE) - jnp.dot(plane_imag, sin_z.T, precision=PRECISE)) * inverse_scale
    return jax.nn.gelu(conv_sum + spectral, approximate=False)
```

```python
import functools
import math

import jax
import jax.numpy as jnp
import numpy as np
from jax import lax
from jax.experimental import pallas as pl
from jax.experimental.pallas import tpu as pltpu
from jax.sharding import PartitionSpec as P

C, NX, NY, NZ = 16, 128, 256, 128
KX, KY, KZ = 24, 24, 12
F32, BF16 = jnp.float32, jnp.bfloat16
MESH = pl.DeviceIdType.MESH

PAIRS_B, PAIRS_C, PAIRS_D = 3, 6, 8


def split(a):
    hi = round_bf16(a)
    return hi, round_bf16(np.asarray(a, np.float64) - hi)


def round_bf16(a):
    import ml_dtypes

    return np.asarray(a, np.float32).astype(ml_dtypes.bfloat16).astype(np.float64)


def bf(a):
    import ml_dtypes

    return np.asarray(a, np.float32).astype(ml_dtypes.bfloat16)


def angles(positions, frequencies, length):
    return 2.0 * math.pi * ((positions[:, None] * frequencies[None, :]) % length) / length


def kept(amount, length):
    index = np.arange(amount)
    return np.where(index < amount // 2, index, length - amount + index)


def tables():
    forward = 1.0 / math.sqrt(NX * NY * NZ)
    inverse = 1.0 / math.sqrt(KX * KY * KZ)
    az = angles(np.arange(NZ), np.arange(KZ), NZ).T
    tz = np.stack([np.cos(az), -np.sin(az)], 1).reshape(2 * KZ, NZ)
    hi, lo = split(tz * forward)
    tzf = np.concatenate([hi, lo, hi], 1)
    pad = np.zeros((8, NZ))
    hi, lo = split(np.concatenate([tz * inverse, pad], 0))
    tzi = np.concatenate([hi, lo, hi], 0)

    qs = kept(KY, NY)
    lyf = np.zeros((16, 96, 96))
    lyi = np.zeros((16, 64, 144))
    for gy in range(16):
        fwd = np.zeros((2, 2, KY, 2, 2, 8))
        inv = np.zeros((2, 2, 2, 8, 2, KY))
        for own in range(2):
            start = 16 * (gy if own == 0 else gy ^ 1)
            for yp in range(2):
                a = angles(start + 2 * np.arange(8) + yp, qs, NY)
                c, s = np.cos(a), np.sin(a)
                fwd[yp, 0, :, own, 0] = c.T
                fwd[yp, 0, :, own, 1] = s.T
                fwd[yp, 1, :, own, 0] = -s.T
                fwd[yp, 1, :, own, 1] = c.T
                re = (c, -s)
                im = (s, c)
                for v in range(2):
                    w = v if yp == 0 else 1 - v
                    inv[yp, 0, own, :, v] = re[w]
                    inv[yp, 1, own, :, v] = im[w]
        hi, lo = split(fwd.reshape(96, 32))
        lyf[gy] = np.concatenate([hi, lo, hi], 1)
        hi, lo = split(inv.reshape(64, 48))
        lyi[gy] = np.concatenate([hi, lo, hi], 1)

    ax = angles(np.arange(NX), kept(KX, NX), NX).reshape(16, 8, KX)
    c = np.broadcast_to(np.cos(ax).transpose(0, 2, 1)[:, :, None, :], (16, KX, 8, 8)).reshape(16, KX, 64)
    s = np.broadcast_to(np.sin(ax).transpose(0, 2, 1)[:, :, None, :], (16, KX, 8, 8)).reshape(16, KX, 64)
    tx = np.stack([np.concatenate([c, s], 2), np.concatenate([-s, c], 2)], 0)

    core, ri, ch, x = np.unravel_index(np.arange(256), (2, 2, 8, 8))
    o, i = np.unravel_index(np.arange(256), (16, 16))
    e1 = (i[None, :] == (core * 8 + ch)[:, None]).astype(np.float64)
    e2 = (o[:, None] == (core * 8 + ch)[None, :]).astype(np.float64)
    i128 = np.arange(128) // 8
    ecol = (np.arange(16)[:, None] == i128[None, :]).astype(np.float64)
    xo = np.arange(8)[:, None]
    xi = (np.arange(128) % 8)[None, :]
    mask = np.stack([(xi - xo == a - 1) for a in range(3)], 0).astype(np.float32)
    eh = np.zeros((2, 16, 128))
    mh = np.zeros((2, 8, 128), np.float32)
    for part, (hi_lo) in enumerate("hlh"):
        for side in range(2):
            lanes = part * 32 + side * 16 + np.arange(16)
            eh[0 if hi_lo == "h" else 1, np.arange(16), lanes] = 1.0
            mh[side, 0 if side == 0 else 7, lanes] = 1.0
    return dict(
        tzf=bf(tzf), tzi=bf(tzi), lyf=bf(lyf), lyi=bf(lyi), tx=tx.astype(np.float32), e1=bf(e1), e2=bf(e2),
        ecol=bf(ecol), eh=bf(eh), mask=mask, mh=mh, eye=np.eye(32, 27, dtype=np.float32),
    )


TABLES = tables()
NAMES = ("tzf", "tzi", "lyf", "lyi", "tx", "e1", "e2", "ecol", "eh", "mask", "mh", "eye")
SMALL = ("tzf", "tzi", "tx", "e1", "e2", "ecol", "eh", "mask", "mh", "eye")


def hilo(v):
    hi = v.astype(BF16)
    return hi, (v - hi.astype(F32)).astype(BF16)


def mm(a, b, dims=(((1,), (0,)), ((), ()))):
    return lax.dot_general(a, b, dims, preferred_element_type=F32)


def erf(x):
    x = jnp.clip(x, -3.832506856900711, 3.832506856900711)
    t = x * x
    p = 0.00022905065861350646
    for coef in (0.0034082910107109506, 0.050955695062380861, 0.18520832239976145, 1.128379143519084):
        p = p * t + coef
    q = -1.1791602954361697e-7
    for coef in (0.000023547966471313185, 0.0010179625278914885, 0.014070470171167667, 0.11098505178285362,
                 0.49746925110067538, 1.0):
        q = q * t + coef
    return x * p / q


def gelu(v):
    return 0.5 * v * (1.0 + erf(v * 0.7071067811865476))


def kernel(f2, f3, w_hbm, cw, tzf, tzi, lyf, lyi, tx, e1, e2, ecol, eh, mask, mh, eye, out_hbm, *refs):
    (fv, wv, cwv, tzf_v, tzi_v, tx_v, e1_v, e2_v, ecol_v, eh_v, mask_v, mh_v, eye_v, lyf_v, lyi_v,
     ws, wb, b, lhs, yh_s, yh, xh, cs, ch, za, zr, ps, pr, rs, rb, co_s, rc, g3, u, ur, co, outv,
     ld, a_s, a_r, h_s, h_r, y_s, y_r, b_s, b_r, c_s, c_r, d_s, d_r, w_s, w_r, u_s, u_r) = refs
    gx = lax.axis_index("gx")
    gy = lax.axis_index("gy")
    y = gy // 4
    jj = gy % 4
    s = gy % 2
    me = gx * 4 + jj
    gxm, gxp = (gx + 15) % 16, (gx + 1) % 16
    gym, gyp = (gy + 15) % 16, (gy + 1) % 16

    loads = [(f2, fv), (w_hbm, wv), (cw, cwv), (lyf.at[gy], lyf_v), (lyi.at[gy], lyi_v), (tzf, tzf_v), (tzi, tzi_v),
             (tx, tx_v), (e1, e1_v), (e2, e2_v), (ecol, ecol_v), (eh, eh_v), (mask, mask_v), (mh, mh_v), (eye, eye_v)]
    copies = [pltpu.make_async_copy(src, dst, ld.at[n]) for n, (src, dst) in enumerate(loads)]
    for copy in copies:
        copy.start()

    barrier = pltpu.get_barrier_semaphore()

    def greet(d, carry):
        @pl.when(d != me)
        def _():
            pl.semaphore_signal(barrier, inc=1, device_id=(d // 4, y * 4 + d % 4), device_id_type=MESH)
        return carry

    lax.fori_loop(0, 64, greet, 0)
    for step in range(1, 4):
        pl.semaphore_signal(barrier, inc=1, device_id=(gx, (gy + 4 * step) % 16), device_id_type=MESH)
    for px in (gxm, gx, gxp):
        for py in (gym, gyp):
            pl.semaphore_signal(barrier, inc=1, device_id=(px, py), device_id_type=MESH)

    b[384:512, :] = jnp.zeros((128, 18 * 128), BF16)
    copies[0].wait()
    for yy in range(16):
        a = jnp.concatenate([fv[pl.ds(c * 128 + yy, 8, stride=16), :] for c in range(16)], 0)
        hi, lo = hilo(a)
        lanes = slice((yy + 1) * 128, (yy + 2) * 128)
        b[0:128, lanes] = hi
        b[128:256, lanes] = lo
        b[256:384, lanes] = hi
        if yy in (0, 15):
            yh_s[0 if yy == 0 else 1] = a
    for n, (x0, y0) in enumerate(((0, 0), (0, 15), (7, 0), (7, 15))):
        cs[n] = jnp.concatenate([fv[pl.ds(c * 128 + x0 * 16 + y0, 1), :] for c in range(16)], 0)

    copies[5].wait()
    for h in range(2):
        for yy in range(8):
            l0 = (2 * yy + 1) * 128
            rows = slice(h * 64, h * 64 + 64)
            lrow = slice(128 + h * 64, 128 + h * 64 + 64)
            hi = jnp.concatenate([b[rows, l0:l0 + 128], b[rows, l0 + 128:l0 + 256]], 0)
            lo = jnp.concatenate([b[lrow, l0:l0 + 128], b[lrow, l0 + 128:l0 + 256]], 0)
            r = mm(tzf_v[...], jnp.concatenate([hi, hi, lo], 1), (((1,), (1,)), ((), ())))
            za[h, pl.ds(yy, 24, stride=8), :] = r

    pl.semaphore_wait(barrier, 72)

    def remote(src, dst, ssem, rsem, px, py):
        return pltpu.make_async_remote_copy(src_ref=src, dst_ref=dst, send_sem=ssem, recv_sem=rsem,
                                            device_id=(px, py), device_id_type=MESH)

    partner = jj + 1 - 2 * s + 4 * y
    ca = remote(za.at[1 - s], zr, a_s, a_r, gx, partner)
    ca.start()

    copies[1].wait()
    copies[14].wait()
    for n in range(4):
        t = lax.dot_general(eye_v[...], wv[pl.ds(128 * n, 128), :], (((1,), (1,)), ((), ())),
                            precision=lax.Precision.HIGHEST, preferred_element_type=F32)
        for m in range(27):
            ws[m, n, :] = t[m, :]

    def owner(r):
        double = r // 64
        return (r - 64 * double) * (1 + 7 * double), double

    def w_copy(m):
        mode = 27 * gx + m
        d, slot = owner(18 * jj + mode % 18)
        p = mode // 18
        return d, slot, p, remote(ws.at[m], wb.at[slot, p], w_s.at[m], w_r.at[slot], d // 4, y * 4 + d % 4)

    def w_send(m, carry):
        d, slot, p, copy = w_copy(m)

        @pl.when(d != me)
        def _():
            copy.start()

        @pl.when(d == me)
        def _():
            pltpu.make_async_copy(ws.at[m], wb.at[slot, p], w_r.at[slot]).start()
        return carry

    lax.fori_loop(0, 27, w_send, 0)

    halos = [
        remote(f3.at[:, pl.ds(112, 16), :], xh.at[0], h_s.at[0], h_r.at[0], gxp, gy),
        remote(f3.at[:, pl.ds(0, 16), :], xh.at[1], h_s.at[1], h_r.at[1], gxm, gy),
        remote(yh_s.at[1], yh.at[0], h_s.at[2], h_r.at[2], gx, gyp),
        remote(yh_s.at[0], yh.at[1], h_s.at[3], h_r.at[3], gx, gym),
        remote(cs.at[0], ch.at[3], h_s.at[4], h_r.at[7], gxm, gym),
        remote(cs.at[1], ch.at[2], h_s.at[5], h_r.at[6], gxm, gyp),
        remote(cs.at[2], ch.at[1], h_s.at[6], h_r.at[5], gxp, gym),
        remote(cs.at[3], ch.at[0], h_s.at[7], h_r.at[4], gxp, gyp),
    ]
    for copy in halos:
        copy.start()

    copies[3].wait()
    ca.wait_recv()
    half = lax.broadcasted_iota(jnp.int32, (24, 128), 1) < 64
    for k in range(12):
        v = jnp.concatenate([za[s, 16 * k:16 * k + 16, :], zr[16 * k:16 * k + 16, :]], 0)
        hi, lo = hilo(v)
        r = mm(lyf_v[...], jnp.concatenate([hi, hi, lo], 0))
        p0 = jnp.where(half, r[0:24], r[72:96])
        p1 = jnp.where(half, r[24:48], r[48:72])
        ps[pl.ds(k, 24, stride=12), :] = p0 + pltpu.roll(p1, 64, 1)

    ycopies = []
    for step in (1, 2, 3):
        yt = (y + step) % 4
        copy = remote(ps.at[pl.ds(pl.multiple_of(yt * 72, 8), 72), :], pr.at[step - 1], y_s.at[step - 1],
                      y_r.at[step - 1], gx, yt * 4 + jj)
        copy.start()
        ycopies.append(copy)
    for n in (2, 10, 11, 12, 13):
        copies[n].wait()
    whi, wlo = hilo(cwv[...])
    ecol_m = ecol_v[...]
    x_hi = mm(whi, ecol_m)
    x_lo = mm(wlo, ecol_m)
    x_h = mm(whi, eh_v[0]) + mm(wlo, eh_v[1])
    masks = [mask_v[a][None] for a in range(3)]

    def spread(v, m, taps):
        total = None
        for t, a in taps:
            term = v[144 * a:144 * a + 144][:, None, :] * m[t]
            total = term if total is None else total + term
        return total.reshape(1152, 128).astype(BF16)

    taps = ((0, 0), (1, 1), (2, 2))
    full_hi = spread(x_hi, masks, taps)
    lhs[:, 0:128] = full_hi
    lhs[:, 128:256] = full_hi
    lhs[:, 256:384] = spread(x_lo, masks, taps)
    lhs[:, 384:512] = spread(x_h, [mh_v[a][None] for a in range(2)], ((0, 0), (1, 2)))

    for copy in ycopies:
        copy.wait_recv()
    own = ps[pl.ds(pl.multiple_of(y * 72, 8), 72), :]
    total = own + pr[0] + pr[1] + pr[2]
    for r in range(72):
        rs[r, :, :] = total[r:r + 1, :]

    def b_send(r, carry):
        d, slot = owner(r)

        @pl.when(d != me)
        def _():
            remote(rs.at[r], rb.at[slot, me], b_s, b_r.at[slot], d // 4, y * 4 + d % 4).start()

        @pl.when(d == me)
        def _():
            pltpu.make_async_copy(rs.at[r], rb.at[slot, me], b_r.at[slot]).start()
        return carry

    lax.fori_loop(0, 72, b_send, 0)
    double = me % 8 == 0

    for copy in halos:
        copy.wait_recv()
    ring = [(0, 0), (17, 1)]
    for yi, side in ring:
        hi, lo = hilo(yh[side])
        lanes = slice(yi * 128, yi * 128 + 128)
        b[0:128, lanes] = hi
        b[128:256, lanes] = lo
        b[256:384, lanes] = hi
    for yi in range(18):
        if yi == 0:
            v = jnp.concatenate([ch[0], ch[2]], 0)
        elif yi == 17:
            v = jnp.concatenate([ch[1], ch[3]], 0)
        else:
            v = jnp.concatenate([xh[side, c, pl.ds(yi - 1, 1), :] for side in range(2) for c in range(16)], 0)
        hi, lo = hilo(v)
        b[384:480, yi * 128:yi * 128 + 128] = jnp.concatenate([hi, hi, lo], 0)

    def conv(pair, carry):
        acc = jnp.zeros((384, 256), F32)
        for t in range(3):
            lanes = pl.ds(pl.multiple_of((2 * pair + t) * 128, 128), 256)
            acc = acc + mm(lhs[384 * t:384 * t + 384, :], b[:, lanes])
        for n in range(2):
            v = acc[:, 128 * n:128 * n + 128]
            v = v[128:256] + pltpu.roll(v[0:128], 1, 1) + pltpu.roll(v[256:384], 127, 1)
            co[pl.ds(pl.multiple_of((2 * pair + n) * 128, 128), 128), :] = v
        return carry

    lax.fori_loop(0, PAIRS_B, conv, 0)

    for n in (7, 8, 9):
        copies[n].wait()

    def mix(slot):
        pltpu.make_async_copy(rb.at[slot], rb.at[slot], b_r.at[slot]).wait()
        pltpu.make_async_copy(wb.at[slot], wb.at[slot], w_r.at[slot]).wait()
        accs = [[jnp.zeros((24, 128), F32) for _ in range(2)] for _ in range(2)]
        for g in range(16):
            for core in range(2):
                row = rb[slot, 4 * g + core] + rb[slot, 4 * g + core + 2]
                row = jnp.broadcast_to(row, (24, 128))
                for part in range(2):
                    accs[part][core] = accs[part][core] + tx_v[part, g] * row
        acc = jnp.concatenate([jnp.concatenate(accs[part], 1) for part in range(2)], 0)
        hi, lo = hilo(acc)
        cc = mm(jnp.concatenate([hi, lo], 0), e1_v[...])
        cc = cc[0:48] + cc[48:96]
        cr, ci = cc[0:24], cc[24:48]
        w4 = [jnp.concatenate([wb[slot, p, pl.ds(n, 1), :] for p in range(24)], 0) for n in range(4)]
        wr = jnp.concatenate(w4[0:2], 1)
        wi = jnp.concatenate(w4[2:4], 1)
        prod = jnp.concatenate([wr * cr - wi * ci, wr * ci + wi * cr], 0)
        hi, lo = hilo(prod)
        mx = mm(jnp.concatenate([hi, lo], 0), e2_v[...])
        mx = mx[0:48] + mx[48:96]
        for core in range(2):
            mr = mx[0:24, 128 * core:128 * core + 128]
            mi = mx[24:48, 128 * core:128 * core + 128]
            for g in range(16):
                row = tx_v[0, g] * mr + tx_v[1, g] * mi
                co_s[slot, 2 * g + core] = jnp.sum(row, axis=0, keepdims=True)

        def c_send(d, carry):
            r = me + slot * 64 if slot == 0 else 64 + me // 8

            @pl.when(d != me)
            def _():
                remote(co_s.at[slot, 2 * (d // 4) + d % 2], rc.at[r], c_s.at[slot], c_r, d // 4,
                       y * 4 + d % 4).start()

            @pl.when(d == me)
            def _():
                pltpu.make_async_copy(co_s.at[slot, 2 * (d // 4) + d % 2], rc.at[r], c_r).start()
            return carry

        lax.fori_loop(0, 64, c_send, 0)

    mix(0)

    @pl.when(double)
    def _():
        mix(1)

    lax.fori_loop(PAIRS_B, PAIRS_C, conv, 0)

    pltpu.make_async_copy(rc, rc, c_r).wait()
    for r in range(72):
        g3[0, r:r + 1, :] = rc[r]
    dcopies = []
    for step in (1, 2, 3):
        yt = (y + step) % 4
        copy = remote(g3.at[0], g3.at[4 - step], d_s.at[step - 1], d_r.at[4 - step], gx, yt * 4 + jj)
        copy.start()
        dcopies.append(copy)
    lax.fori_loop(PAIRS_C, PAIRS_D, conv, 0)
    copies[4].wait()
    for n in range(1, 4):
        pltpu.make_async_copy(g3.at[n], g3.at[n], d_r.at[n]).wait()

    half16 = lax.broadcasted_iota(jnp.int32, (16, 128), 1) < 64
    u[:, :, 24:32, :] = jnp.zeros((2, 8, 8, 128), F32)
    for k in range(12):
        v = jnp.concatenate([g3[(t - y) % 4, pl.ds(k, 6, stride=12), :] for t in range(4)], 0)
        v = jnp.concatenate([v, pltpu.roll(v, 64, 1)], 0)
        hi, lo = hilo(v)
        r = mm(lyi_v[...], jnp.concatenate([hi, hi, lo], 0))
        for part in range(2):
            v = jnp.where(half16, r[16 * part:16 * part + 16], r[32 + 16 * part:48 + 16 * part])
            for dst in range(2):
                for yy in range(8):
                    u[dst, yy, pl.ds(2 * k + part, 1), :] = v[8 * dst + yy:8 * dst + yy + 1]

    cu = remote(u.at[1], ur, u_s, u_r, gx, partner)
    cu.start()

    copies[6].wait()

    def finish(v, hh, yy):
        hi, lo = hilo(v)
        r = mm(jnp.concatenate([hi, hi, lo], 0), tzi_v[...], (((0,), (0,)), ((), ())))
        for yp in range(2):
            yr = 2 * yy + yp
            base = pl.multiple_of(yr * 128 + hh * 64, 64)
            t = gelu(r[64 * yp:64 * yp + 64] + co[pl.ds(base, 64), :])
            for c in range(8):
                outv[pl.ds(hh * 1024 + c * 128 + yr, 8, stride=16), :] = t[8 * c:8 * c + 8]

    for yy in range(8):
        finish(u[0, yy], s, yy)
    cu.wait_recv()
    for yy in range(8):
        finish(ur[yy], 1 - s, yy)
    store = pltpu.make_async_copy(outv, out_hbm, ld.at[15])
    store.start()

    ca.wait_send()
    cu.wait_send()
    for copy in halos + ycopies + dcopies:
        copy.wait_send()

    def w_done(m, carry):
        d, slot, p, copy = w_copy(m)

        @pl.when(d != me)
        def _():
            copy.wait_send()
        return carry

    lax.fori_loop(0, 27, w_done, 0)

    def sent(sem, rows):
        part = rs.at[pl.ds(0, rows)]
        pltpu.make_async_copy(part, part, sem).wait()

    @pl.when(double)
    def _():
        sent(b_s, 70)
        sent(c_s.at[1], 63)

    @pl.when(jnp.logical_not(double))
    def _():
        sent(b_s, 71)

    sent(c_s.at[0], 63)
    store.wait()


def shards(features, conv_weight, mix_weight):
    f2 = features.reshape(2048, 128)
    f3 = features.reshape(16, 128, 128)
    w = mix_weight.reshape(512, 27)
    cw = conv_weight.reshape(432, 16)
    consts = [jnp.asarray(TABLES[n]) for n in NAMES]
    vm = pltpu.VMEM
    dma = pltpu.SemaphoreType.DMA
    scratch = [
        vm((2048, 128), F32), vm((512, 27), F32), vm((432, 16), F32),
        vm((24, 384), BF16), vm((96, 128), BF16), vm((2, 16, 24, 128), F32), vm((256, 256), BF16), vm((256, 256), BF16),
        vm((16, 128), BF16), vm((2, 16, 128), BF16), vm((3, 8, 128), F32), vm((2, 8, 128), F32), vm((32, 27), F32),
        vm((96, 96), BF16), vm((64, 144), BF16),
        vm((27, 4, 128), F32), vm((2, 24, 4, 128), F32), vm((512, 18 * 128), BF16), vm((1152, 512), BF16),
        vm((2, 128, 128), F32), vm((2, 128, 128), F32), vm((2, 16, 16, 128), F32), vm((4, 16, 128), F32),
        vm((4, 16, 128), F32), vm((2, 192, 128), F32), vm((192, 128), F32), vm((288, 128), F32), vm((3, 72, 128), F32),
        vm((72, 1, 128), F32), vm((2, 64, 1, 128), F32), vm((2, 32, 1, 128), F32), vm((72, 1, 128), F32),
        vm((4, 72, 128), F32), vm((2, 8, 32, 128), F32), vm((8, 32, 128), F32), vm((2048, 128), F32),
        vm((2048, 128), F32),
        dma((16,)), dma, dma, dma((8,)), dma((8,)), dma((3,)), dma((3,)), dma, dma((2,)), dma((2,)), dma,
        dma((3,)), dma((4,)), dma((27,)), dma((2,)), dma, dma,
    ]
    any_spec = pl.BlockSpec(memory_space=pl.ANY)
    out = pl.pallas_call(
        kernel,
        out_shape=jax.ShapeDtypeStruct((2048, 128), F32),
        in_specs=[any_spec] * (4 + len(NAMES)),
        out_specs=any_spec,
        scratch_shapes=scratch,
        compiler_params=pltpu.CompilerParams(collective_id=0, has_side_effects=True,
                                             vmem_limit_bytes=56 * 1024 * 1024),
        name="layer",
    )(f2, f3, w, cw, *consts)
    return out.reshape(features.shape)


def solution(mesh):
    in_specs = (P(None, "gx", "gy", None), P(), P(None, None, None, "gy", "gx"))
    return jax.shard_map(shards, mesh=mesh, in_specs=in_specs, out_specs=P(None, "gx", "gy", None), check_vma=False)
```

```python
import functools
import math

import jax
import jax.numpy as jnp
import numpy as np
from jax import lax
from jax.experimental import pallas as pl
from jax.experimental.pallas import tpu as pltpu
from jax.sharding import PartitionSpec as P

C, NX, NY, NZ = 16, 128, 256, 128
KX, KY, KZ = 24, 24, 12
F32, BF16 = jnp.float32, jnp.bfloat16
MESH = pl.DeviceIdType.MESH


def split(a):
    hi = round_bf16(a)
    return hi, round_bf16(np.asarray(a, np.float64) - hi)


def round_bf16(a):
    import ml_dtypes

    return np.asarray(a, np.float32).astype(ml_dtypes.bfloat16).astype(np.float64)


def bf(a):
    import ml_dtypes

    return np.asarray(a, np.float32).astype(ml_dtypes.bfloat16)


def angles(positions, frequencies, length):
    return 2.0 * math.pi * ((positions[:, None] * frequencies[None, :]) % length) / length


def kept(amount, length):
    index = np.arange(amount)
    return np.where(index < amount // 2, index, length - amount + index)


def tables():
    forward = 1.0 / math.sqrt(NX * NY * NZ)
    inverse = 1.0 / math.sqrt(KX * KY * KZ)
    az = angles(np.arange(NZ), np.arange(KZ), NZ).T
    tz = np.stack([np.cos(az), -np.sin(az)], 1).reshape(2 * KZ, NZ)
    hi, lo = split(tz * forward)
    tzf = np.concatenate([hi, lo, hi], 1)
    pad = np.zeros((8, NZ))
    hi, lo = split(np.concatenate([tz * inverse, pad], 0))
    tzi = np.concatenate([hi, lo, hi], 0)

    qs = kept(KY, NY)
    lyf = np.zeros((16, 96, 96))
    lyi = np.zeros((16, 64, 192))
    for gy in range(16):
        fwd = np.zeros((2, 2, KY, 2, 2, 8))
        inv = np.zeros((2, 2, 2, 8, 2, KY))
        for own in range(2):
            start = 16 * (gy if own == 0 else gy ^ 1)
            for yp in range(2):
                a = angles(start + 2 * np.arange(8) + yp, qs, NY)
                c, s = np.cos(a), np.sin(a)
                fwd[yp, 0, :, own, 0] = c.T
                fwd[yp, 0, :, own, 1] = s.T
                fwd[yp, 1, :, own, 0] = -s.T
                fwd[yp, 1, :, own, 1] = c.T
                re = (c, -s)
                im = (s, c)
                for v in range(2):
                    w = v if yp == 0 else 1 - v
                    inv[yp, 0, own, :, v] = re[w]
                    inv[yp, 1, own, :, v] = im[w]
        hi, lo = split(fwd.reshape(96, 32))
        lyf[gy] = np.concatenate([hi, lo, hi], 1)
        inv = np.concatenate([inv.reshape(64, 2, 4, 6), np.zeros((64, 2, 4, 2))], 3)
        hi, lo = split(inv.reshape(64, 64))
        lyi[gy] = np.concatenate([hi, lo, hi], 1)

    ax = angles(np.arange(NX), kept(KX, NX), NX).reshape(16, 8, KX)
    c = np.broadcast_to(np.cos(ax).transpose(0, 2, 1)[:, :, None, :], (16, KX, 8, 8)).reshape(16, KX, 64)
    s = np.broadcast_to(np.sin(ax).transpose(0, 2, 1)[:, :, None, :], (16, KX, 8, 8)).reshape(16, KX, 64)
    tx = np.stack([np.concatenate([c, s], 2), np.concatenate([-s, c], 2)], 0)

    core, ri, ch, x = np.unravel_index(np.arange(256), (2, 2, 8, 8))
    o, i = np.unravel_index(np.arange(256), (16, 16))
    e1 = (i[None, :] == (core * 8 + ch)[:, None]).astype(np.float64)
    e2 = (o[:, None] == (core * 8 + ch)[None, :]).astype(np.float64)
    i128 = np.arange(128) // 8
    ecol = (np.arange(256)[:, None] % 16 == i128[None, :]).astype(np.float64)
    xo = np.arange(8)[:, None]
    xi = (np.arange(128) % 8)[None, :]
    mask = np.stack([(xi - xo == a - 1) for a in range(3)], 0).astype(np.float32)
    eh = np.zeros((2, 256, 128))
    mh = np.zeros((3, 8, 128), np.float32)
    for part, (hi_lo) in enumerate("hlh"):
        for side in range(2):
            lanes = part * 32 + side * 16 + np.arange(16)
            eh[0 if hi_lo == "h" else 1, np.arange(256), lanes[np.arange(256) % 16]] = 1.0
            mh[2 * side, 0 if side == 0 else 7, lanes] = 1.0
    return dict(
        tzf=bf(tzf), tzi=bf(tzi), lyf=bf(lyf), lyi=bf(lyi), tx=tx.astype(np.float32), e1=bf(e1), e2=bf(e2),
        ecol=bf(ecol), eh=bf(eh), mask=mask, mh=mh, eye=np.eye(32, 27, dtype=np.float32),
    )


TABLES = tables()
NAMES = ("tzf", "tzi", "lyf", "lyi", "tx", "e1", "e2", "ecol", "eh", "mask", "mh", "eye")


def hilo(v):
    hi = v.astype(BF16)
    return hi, (v - hi.astype(F32)).astype(BF16)


def mm(a, b, dims=(((1,), (0,)), ((), ()))):
    return lax.dot_general(a, b, dims, preferred_element_type=F32)


def erf(x):
    x = jnp.clip(x, -3.832506856900711, 3.832506856900711)
    t = x * x
    p = 0.00022905065861350646
    for coef in (0.0034082910107109506, 0.050955695062380861, 0.18520832239976145, 1.128379143519084):
        p = p * t + coef
    q = -1.1791602954361697e-7
    for coef in (0.000023547966471313185, 0.0010179625278914885, 0.014070470171167667, 0.11098505178285362,
                 0.49746925110067538, 1.0):
        q = q * t + coef
    return x * p / q


def gelu(v):
    return 0.5 * v * (1.0 + erf(v * 0.7071067811865476))


FAR_Z = (4, 3, 5, 2, 6, 1, 7, 0)
FAR_X = (2, 1, 3, 0)


def kernel(f2, f3, w_hbm, cw, tzf, tzi, lyf, lyi, tx, e1, e2, ecol, eh, mask, mh, eye, v_out, *refs):
    (fv, wv, cwv, tzf_v, tzi_v, tx_v, e1_v, e2_v, ecol_v, eh_v, mask_v, mh_v, eye_v, lyf_v, lyi_v,
     ws, wb, b, lhs, xs, yh_s, yh, xh, cs, ch, za, zr, ps, pr, rs, rb, co_s, rc, g3, u, ur,
     ld, a_s, a_r, h_s, h_r, y_s, y_r, b_s, b_r, c_s, c_r, d_s, d_r, w_s, w_r, u_s, u_r) = refs
    gx = lax.axis_index("gx")
    gy = lax.axis_index("gy")
    y = gy // 4
    jj = gy % 4
    s = gy % 2
    x = gx % 4
    z = (gx // 4) + 4 * (jj // 2)
    me = gx * 4 + jj
    gxm, gxp = (gx + 15) % 16, (gx + 1) % 16
    gym, gyp = (gy + 15) % 16, (gy + 1) % 16

    loads = [(f2, fv), (w_hbm, wv), (cw, cwv), (lyf.at[gy], lyf_v), (lyi.at[gy], lyi_v), (tzf, tzf_v), (tzi, tzi_v),
             (tx, tx_v), (e1, e1_v), (e2, e2_v), (ecol, ecol_v), (eh, eh_v), (mask, mask_v), (mh, mh_v), (eye, eye_v)]
    copies = [pltpu.make_async_copy(src, dst, ld.at[n]) for n, (src, dst) in enumerate(loads)]
    for n in (0, 5):
        copies[n].start()

    xs4 = [(x + dx) % 4 for dx in FAR_X]
    peers = []
    for dz in FAR_Z:
        zz = (z + dz) % 8
        base, hi2 = (zz % 4) * 4, (zz // 4) * 2
        for n, dx in enumerate(FAR_X):
            for dc in (1, 0):
                if dz or dx or dc:
                    peers.append((base + xs4[n], hi2 + (s + dc) % 2))

    barrier = pltpu.get_barrier_semaphore()

    def greet(px, py):
        pl.semaphore_signal(barrier, inc=1, device_id=(px, py), device_id_type=MESH)

    for px in (gxm, gx, gxp):
        for py in (gym, gyp):
            greet(px, py)
    for px, pj in peers:
        greet(px, 4 * y + pj)
    for step in (2, 1, 3):
        greet(gx, (gy + 4 * step) % 16)
    for n in (3, 1, 14, 2, 10, 11, 12, 13, 7, 8, 9, 4, 6):
        copies[n].start()

    copies[0].wait()
    for yy in range(16):
        a = jnp.concatenate([fv[pl.ds(c * 128 + yy, 8, stride=16), :] for c in range(16)], 0)
        hi, lo = hilo(a)
        lanes = slice((yy + 1) * 128, (yy + 2) * 128)
        b[0:128, lanes] = hi
        b[128:256, lanes] = lo
        b[256:384, lanes] = hi
        if yy in (0, 15):
            yh_s[0 if yy == 0 else 1] = a

    copies[5].wait()

    def along_z(h):
        r0 = pl.multiple_of(h * 64, 64)
        for yy in range(8):
            l0 = (2 * yy + 1) * 128
            hi = jnp.concatenate([b[pl.ds(r0, 64), l0:l0 + 128], b[pl.ds(r0, 64), l0 + 128:l0 + 256]], 0)
            lo = jnp.concatenate([b[pl.ds(r0 + 128, 64), l0:l0 + 128], b[pl.ds(r0 + 128, 64), l0 + 128:l0 + 256]], 0)
            r = mm(tzf_v[...], jnp.concatenate([hi, hi, lo], 1), (((1,), (1,)), ((), ())))
            za[h, pl.ds(yy, 24, stride=8), :] = r

    along_z(1 - s)
    pl.semaphore_wait(barrier, 72)

    def remote(src, dst, ssem, rsem, px, py):
        return pltpu.make_async_remote_copy(src_ref=src, dst_ref=dst, send_sem=ssem, recv_sem=rsem,
                                            device_id=(px, py), device_id_type=MESH)

    partner = jj + 1 - 2 * s + 4 * y
    acopies = [remote(za.at[1 - s, pl.ds(48 * n, 48)], zr.at[pl.ds(48 * n, 48)], a_s.at[n], a_r.at[n], gx, partner)
               for n in range(4)]
    for copy in acopies:
        copy.start()
    halos = [
        remote(f3.at[:, pl.ds(112, 16), :], xh.at[0], h_s.at[0], h_r.at[0], gxp, gy),
        remote(f3.at[:, pl.ds(0, 16), :], xh.at[1], h_s.at[1], h_r.at[1], gxm, gy),
    ]
    for copy in halos:
        copy.start()
    along_z(s)

    copies[1].wait()
    copies[14].wait()
    for n in range(4):
        t = lax.dot_general(eye_v[...], wv[pl.ds(128 * n, 128), :], (((1,), (1,)), ((), ())),
                            precision=lax.Precision.HIGHEST, preferred_element_type=F32)
        for m in range(27):
            ws[m, n, :] = t[m, :]

    copies[3].wait()
    half = lax.broadcasted_iota(jnp.int32, (24, 128), 1) < 64
    for k in range(12):
        if k % 3 == 0:
            acopies[k // 3].wait_recv()
        v = jnp.concatenate([za[s, 16 * k:16 * k + 16, :], zr[16 * k:16 * k + 16, :]], 0)
        hi, lo = hilo(v)
        r = mm(lyf_v[...], jnp.concatenate([hi, hi, lo], 0))
        p0 = jnp.where(half, r[0:24], r[72:96])
        p1 = jnp.where(half, r[24:48], r[48:72])
        ps[pl.ds(k, 24, stride=12), :] = p0 + pltpu.roll(p1, 64, 1)

    ycopies = []
    for step in (2, 1, 3):
        yt = (y + step) % 4
        copy = remote(ps.at[pl.ds(pl.multiple_of(yt * 72, 8), 72), :], pr.at[step - 1], y_s.at[step - 1],
                      y_r.at[step - 1], gx, yt * 4 + jj)
        copy.start()
        ycopies.append(copy)

    def w_copy(m):
        mode = 27 * gx + m
        r = 18 * jj + mode % 18
        d = 8 * (r // 9) + jnp.maximum(r % 9 - 1, 0)
        slot = (r % 9 == 1).astype(jnp.int32)
        p = mode // 18
        return d, slot, p, remote(ws.at[m], wb.at[slot, p], w_s.at[m], w_r.at[slot], d // 4, y * 4 + d % 4)

    def w_send(m, carry):
        d, slot, p, copy = w_copy(m)

        @pl.when(d != me)
        def _():
            copy.start()

        @pl.when(d == me)
        def _():
            pltpu.make_async_copy(ws.at[m], wb.at[slot, p], w_r.at[slot]).start()
        return carry

    lax.fori_loop(0, 27, w_send, 0)

    for n, (x0, y0) in enumerate(((0, 0), (0, 15), (7, 0), (7, 15))):
        cs[n] = jnp.concatenate([fv[pl.ds(c * 128 + x0 * 16 + y0, 1), :] for c in range(16)], 0)
    more = [
        remote(yh_s.at[1], yh.at[0], h_s.at[2], h_r.at[2], gx, gyp),
        remote(yh_s.at[0], yh.at[1], h_s.at[3], h_r.at[3], gx, gym),
        remote(cs.at[0], ch.at[3], h_s.at[4], h_r.at[7], gxm, gym),
        remote(cs.at[1], ch.at[2], h_s.at[5], h_r.at[6], gxm, gyp),
        remote(cs.at[2], ch.at[1], h_s.at[6], h_r.at[5], gxp, gym),
        remote(cs.at[3], ch.at[0], h_s.at[7], h_r.at[4], gxp, gyp),
    ]
    for copy in more:
        copy.start()
    halos = halos + more
    rs[72] = jnp.zeros((1, 128), F32)

    for copy in ycopies:
        copy.wait_recv()
    total = ps[pl.ds(pl.multiple_of(y * 72, 8), 72), :] + pr[0] + pr[1] + pr[2]
    for r in range(72):
        rs[r, :, :] = total[r:r + 1, :]

    def b_copy(px, pj):
        d = px * 4 + pj
        u8 = d % 8
        r = 9 * (d // 8) + u8 + (u8 > 0).astype(jnp.int32)
        return rs.at[pl.ds(r, 2)], px, 4 * y + pj

    for px, pj in peers:
        src, dx, dy = b_copy(px, pj)
        remote(src, rb.at[me], b_s, b_r, dx, dy).start()
    src, _, _ = b_copy(gx, jj)
    pltpu.make_async_copy(src, rb.at[me], b_r).start()
    double = me % 8 == 0

    for n in (2, 10, 11, 12, 13):
        copies[n].wait()
    cwt = lax.dot_general(eye_v[...], cwv[...], (((1,), (1,)), ((), ())),
                          precision=lax.Precision.HIGHEST, preferred_element_type=F32)
    group = lax.broadcasted_iota(jnp.int32, (32, 256), 1) // 16
    picked = jnp.concatenate([jnp.where(group == o, cwt, 0.0) for o in range(16)], 0)
    whi, wlo = hilo(picked)
    xs[0] = mm(whi, ecol_v[...])
    xs[1] = mm(wlo, ecol_v[...])
    xs[2] = mm(whi, eh_v[0]) + mm(wlo, eh_v[1])

    def spread(op, carry):
        for t in range(3):
            ms = [mask_v[a] > 0 if t < 2 else mh_v[a] > 0 for a in range(3)]
            for yb in range(3):
                parts = []
                for oo in range(2):
                    for zc in range(3):
                        v = jnp.zeros((8, 128), F32)
                        for a in range(3) if t < 2 else (0, 2):
                            row = xs[t, pl.ds((2 * op + oo) * 32 + 9 * a + 3 * yb + zc, 1), :]
                            v = jnp.where(ms[a], jnp.broadcast_to(row, (8, 128)), v)
                        parts.append(v)
                v = jnp.concatenate(parts, 0).astype(BF16)
                rows = pl.ds(pl.multiple_of(384 * yb + 48 * op, 16), 48)
                if t == 0:
                    lhs[rows, 0:128] = v
                    lhs[rows, 128:256] = v
                else:
                    lhs[rows, 128 + 128 * t:256 + 128 * t] = v
        return carry

    lax.fori_loop(0, 8, spread, 0)

    b[384:512, :] = jnp.zeros((128, 18 * 128), BF16)
    for copy in halos:
        copy.wait_recv()
    for yi, side in ((0, 0), (17, 1)):
        hi, lo = hilo(yh[side])
        lanes = slice(yi * 128, yi * 128 + 128)
        b[0:128, lanes] = hi
        b[128:256, lanes] = lo
        b[256:384, lanes] = hi
    for yi in range(18):
        if yi == 0:
            v = jnp.concatenate([ch[0], ch[2]], 0)
        elif yi == 17:
            v = jnp.concatenate([ch[1], ch[3]], 0)
        else:
            v = jnp.concatenate([xh[side, c, pl.ds(yi - 1, 1), :] for side in range(2) for c in range(16)], 0)
        hi, lo = hilo(v)
        b[384:480, yi * 128:yi * 128 + 128] = jnp.concatenate([hi, hi, lo], 0)

    def conv(pair, carry):
        acc = jnp.zeros((384, 256), F32)
        for t in range(3):
            lanes = pl.ds(pl.multiple_of((2 * pair + t) * 128, 128), 256)
            acc = acc + mm(lhs[384 * t:384 * t + 384, :], b[:, lanes])
        for n in range(2):
            v = acc[:, 128 * n:128 * n + 128].reshape(16, 3, 8, 128)
            v0, v1, v2 = (v[:, i].reshape(128, 128) for i in range(3))
            v = v1 + pltpu.roll(v0, 1, 1) + pltpu.roll(v2, 127, 1)
            v_out[pl.ds(pl.multiple_of((2 * pair + n) * 128, 128), 128), :] = v
        return carry

    for n in (7, 8, 9):
        copies[n].wait()
    pltpu.make_async_copy(wb.at[0], wb.at[0], w_r.at[0]).wait()

    @pl.when(double)
    def _():
        pltpu.make_async_copy(wb.at[1], wb.at[1], w_r.at[1]).wait()

    pltpu.make_async_copy(rb, rb, b_r).wait()

    def mix(slots):
        accs = [[[jnp.zeros((24, 128), F32) for _ in range(2)] for _ in range(2)] for _ in slots]
        for g in range(16):
            for core in range(2):
                for n, slot in enumerate(slots):
                    row = rb[4 * g + core, slot] + rb[4 * g + core + 2, slot]
                    row = jnp.broadcast_to(row, (24, 128))
                    for part in range(2):
                        accs[n][part][core] = accs[n][part][core] + tx_v[part, g] * row
        acc = jnp.concatenate([jnp.concatenate(accs[n][part], 1) for n in range(len(slots)) for part in range(2)], 0)
        size = 48 * len(slots)
        hi, lo = hilo(acc)
        cc = mm(jnp.concatenate([hi, lo], 0), e1_v[...])
        cc = cc[0:size] + cc[size:2 * size]
        prods = []
        for n, slot in enumerate(slots):
            cr, ci = cc[48 * n:48 * n + 24], cc[48 * n + 24:48 * n + 48]
            w4 = [jnp.concatenate([wb[slot, p, pl.ds(t, 1), :] for p in range(24)], 0) for t in range(4)]
            wr = jnp.concatenate(w4[0:2], 1)
            wi = jnp.concatenate(w4[2:4], 1)
            prods += [wr * cr - wi * ci, wr * ci + wi * cr]
        hi, lo = hilo(jnp.concatenate(prods, 0))
        mx = mm(jnp.concatenate([hi, lo], 0), e2_v[...])
        mx = mx[0:size] + mx[size:2 * size]
        for g in range(16):
            for core in range(2):
                for n, slot in enumerate(slots):
                    lanes = slice(128 * core, 128 * core + 128)
                    row = tx_v[0, g] * mx[48 * n:48 * n + 24, lanes] + tx_v[1, g] * mx[48 * n + 24:48 * n + 48, lanes]
                    co_s[2 * g + core, slot] = jnp.sum(row, axis=0, keepdims=True)
                if len(slots) == 1:
                    co_s[2 * g + core, 1] = jnp.zeros((1, 128), F32)

    @pl.when(double)
    def _():
        mix((0, 1))

    @pl.when(jnp.logical_not(double))
    def _():
        mix((0,))

    for px, pj in peers:
        remote(co_s.at[2 * px + pj % 2], rc.at[me], c_s, c_r, px, 4 * y + pj).start()
    pltpu.make_async_copy(co_s.at[2 * gx + s], rc.at[me], c_r).start()

    lax.fori_loop(0, 8, conv, 0)

    for t in range(4):
        g3[t, 72:96, :] = jnp.zeros((24, 128), F32)
    pltpu.make_async_copy(rc, rc, c_r).wait()
    for r in range(72):
        t8, u8 = r // 9, r % 9
        g3[0, r:r + 1, :] = rc[8 * t8 + max(u8 - 1, 0), 1 if u8 == 1 else 0]
    dcopies = []
    for step in (2, 1, 3):
        yt = (y + step) % 4
        copy = remote(g3.at[0, pl.ds(0, 72)], g3.at[4 - step, pl.ds(0, 72)], d_s.at[step - 1], d_r.at[4 - step],
                      gx, yt * 4 + jj)
        copy.start()
        dcopies.append(copy)
    copies[4].wait()
    copies[6].wait()
    for copy in dcopies:
        copy.wait_recv()

    half16 = lax.broadcasted_iota(jnp.int32, (16, 128), 1) < 64
    for k in range(12):
        v = jnp.concatenate([g3[(t - y + 4) % 4, pl.ds(k, 8, stride=12), :] for t in range(4)], 0)
        v = jnp.concatenate([v, pltpu.roll(v, 64, 1)], 0)
        hi, lo = hilo(v)
        r = mm(lyi_v[...], jnp.concatenate([hi, hi, lo], 0))
        for part in range(2):
            v = jnp.where(half16, r[16 * part:16 * part + 16], r[32 + 16 * part:48 + 16 * part])
            for dst in range(2):
                u[dst, pl.ds(2 * k + part, 8, stride=24), :] = v[8 * dst:8 * dst + 8]

    ucopies = [remote(u.at[1, pl.ds(48 * n, 48)], ur.at[pl.ds(48 * n, 48)], u_s.at[n], u_r.at[n], gx, partner)
               for n in range(4)]
    for copy in ucopies:
        copy.start()

    zero8 = jnp.zeros((8, 128), F32)

    def finish(v, hh, yy):
        hi, lo = hilo(jnp.concatenate([v, zero8], 0))
        r = mm(jnp.concatenate([hi, hi, lo], 0), tzi_v[...], (((0,), (0,)), ((), ())))
        for yp in range(2):
            rows = pl.ds(pl.multiple_of((2 * yy + yp) * 128 + hh * 64, 64), 64)
            v_out[rows, :] = v_out[rows, :] + r[64 * yp:64 * yp + 64]

    for yy in range(8):
        finish(u[0, 24 * yy:24 * yy + 24, :], s, yy)
    for yy in range(8):
        if yy % 2 == 0:
            ucopies[yy // 2].wait_recv()
        finish(ur[24 * yy:24 * yy + 24, :], 1 - s, yy)

    for copy in acopies + ucopies + halos + ycopies + dcopies:
        copy.wait_send()

    def w_done(m, carry):
        d, slot, p, copy = w_copy(m)

        @pl.when(d != me)
        def _():
            copy.wait_send()
        return carry

    lax.fori_loop(0, 27, w_done, 0)
    part = rb.at[pl.ds(0, 63)]
    pltpu.make_async_copy(part, part, b_s).wait()
    pltpu.make_async_copy(part, part, c_s).wait()


def gelu_kernel(v, out_hbm, outv, sem):
    copies = []
    for n in range(4):
        for yr in range(16):
            t = gelu(v[yr * 128 + 32 * n:yr * 128 + 32 * n + 32, :])
            for c in range(4):
                outv[pl.ds((4 * n + c) * 128 + yr, 8, stride=16), :] = t[8 * c:8 * c + 8]
        rows = pl.ds(512 * n, 512)
        copy = pltpu.make_async_copy(outv.at[rows], out_hbm.at[rows], sem.at[n])
        copy.start()
        copies.append(copy)
    for copy in copies:
        copy.wait()


def shards(features, conv_weight, mix_weight):
    f2 = features.reshape(2048, 128)
    f3 = features.reshape(16, 128, 128)
    w = mix_weight.reshape(512, 27)
    cw = conv_weight.transpose(1, 2, 0).reshape(256, 27)
    consts = [jnp.asarray(TABLES[n]) for n in NAMES]
    vm = pltpu.VMEM
    dma = pltpu.SemaphoreType.DMA
    scratch = [
        vm((2048, 128), F32), vm((512, 27), F32), vm((256, 27), F32),
        vm((24, 384), BF16), vm((96, 128), BF16), vm((2, 16, 24, 128), F32), vm((256, 256), BF16), vm((256, 256), BF16),
        vm((256, 128), BF16), vm((2, 256, 128), BF16), vm((3, 8, 128), F32), vm((3, 8, 128), F32), vm((32, 27), F32),
        vm((96, 96), BF16), vm((64, 192), BF16),
        vm((27, 4, 128), F32), vm((2, 24, 4, 128), F32), vm((512, 18 * 128), BF16), vm((1152, 512), BF16),
        vm((3, 512, 128), F32),
        vm((2, 128, 128), F32), vm((2, 128, 128), F32), vm((2, 16, 16, 128), F32), vm((4, 16, 128), F32),
        vm((4, 16, 128), F32), vm((2, 192, 128), F32), vm((192, 128), F32), vm((288, 128), F32), vm((3, 72, 128), F32),
        vm((73, 1, 128), F32), vm((64, 2, 1, 128), F32), vm((32, 2, 1, 128), F32), vm((64, 2, 1, 128), F32),
        vm((4, 96, 128), F32), vm((2, 192, 128), F32), vm((192, 128), F32),
        dma((15,)), dma((4,)), dma((4,)), dma((8,)), dma((8,)), dma((3,)), dma((3,)), dma, dma, dma, dma,
        dma((3,)), dma((4,)), dma((27,)), dma((2,)), dma((4,)), dma((4,)),
    ]
    any_spec = pl.BlockSpec(memory_space=pl.ANY)
    vmem_spec = pl.BlockSpec(memory_space=pltpu.VMEM)
    hbm_spec = pl.BlockSpec(memory_space=pltpu.HBM)
    v = pl.pallas_call(
        kernel,
        out_shape=jax.ShapeDtypeStruct((2048, 128), F32),
        in_specs=[hbm_spec] * (4 + len(NAMES)),
        out_specs=vmem_spec,
        scratch_shapes=scratch,
        compiler_params=pltpu.CompilerParams(collective_id=0, has_side_effects=True,
                                             vmem_limit_bytes=40 * 1024 * 1024),
        name="layer",
    )(*[pltpu.with_memory_space_constraint(a, pltpu.HBM) for a in (f2, f3, w, cw, *consts)])
    out = pl.pallas_call(
        gelu_kernel,
        out_shape=jax.ShapeDtypeStruct((2048, 128), F32),
        in_specs=[vmem_spec],
        out_specs=any_spec,
        scratch_shapes=[vm((2048, 128), F32), dma((4,))],
        compiler_params=pltpu.CompilerParams(vmem_limit_bytes=8 * 1024 * 1024),
        name="act",
    )(v)
    return out.reshape(features.shape)


def solution(mesh):
    in_specs = (P(None, "gx", "gy", None), P(), P(None, None, None, "gy", "gx"))
    return jax.shard_map(shards, mesh=mesh, in_specs=in_specs, out_specs=P(None, "gx", "gy", None), check_vma=False)
```

```python
import functools
import math

import jax
import jax.numpy as jnp
import numpy as np
from jax import lax
from jax.experimental import pallas as pl
from jax.experimental.pallas import tpu as pltpu
from jax.sharding import PartitionSpec as P

C, NX, NY, NZ = 16, 128, 256, 128
KX, KY, KZ = 24, 24, 12
F32, BF16 = jnp.float32, jnp.bfloat16
MESH = pl.DeviceIdType.MESH


def split(a):
    hi = round_bf16(a)
    return hi, round_bf16(np.asarray(a, np.float64) - hi)


def round_bf16(a):
    import ml_dtypes

    return np.asarray(a, np.float32).astype(ml_dtypes.bfloat16).astype(np.float64)


def bf(a):
    import ml_dtypes

    return np.asarray(a, np.float32).astype(ml_dtypes.bfloat16)


def angles(positions, frequencies, length):
    return 2.0 * math.pi * ((positions[:, None] * frequencies[None, :]) % length) / length


def kept(amount, length):
    index = np.arange(amount)
    return np.where(index < amount // 2, index, length - amount + index)


def tables():
    forward = 1.0 / math.sqrt(NX * NY * NZ)
    inverse = 1.0 / math.sqrt(KX * KY * KZ)
    az = angles(np.arange(NZ), np.arange(KZ), NZ).T
    tz = np.stack([np.cos(az), -np.sin(az)], 1).reshape(2 * KZ, NZ)
    hi, lo = split(tz * forward)
    tzf = np.concatenate([hi, lo, hi], 1)
    pad = np.zeros((8, NZ))
    hi, lo = split(np.concatenate([tz * inverse, pad], 0))
    tzi = np.concatenate([hi, lo, hi], 0)

    qs = kept(KY, NY)
    lyf = np.zeros((16, 96, 96))
    lyi = np.zeros((16, 64, 192))
    for gy in range(16):
        fwd = np.zeros((2, 2, KY, 2, 2, 8))
        inv = np.zeros((2, 2, 2, 8, 2, KY))
        for own in range(2):
            start = 16 * (gy if own == 0 else gy ^ 1)
            for yp in range(2):
                a = angles(start + 2 * np.arange(8) + yp, qs, NY)
                c, s = np.cos(a), np.sin(a)
                fwd[yp, 0, :, own, 0] = c.T
                fwd[yp, 0, :, own, 1] = s.T
                fwd[yp, 1, :, own, 0] = -s.T
                fwd[yp, 1, :, own, 1] = c.T
                re = (c, -s)
                im = (s, c)
                for v in range(2):
                    w = v if yp == 0 else 1 - v
                    inv[yp, 0, own, :, v] = re[w]
                    inv[yp, 1, own, :, v] = im[w]
        hi, lo = split(fwd.reshape(96, 32))
        lyf[gy] = np.concatenate([hi, lo, hi], 1)
        inv = np.concatenate([inv.reshape(64, 2, 4, 6), np.zeros((64, 2, 4, 2))], 3)
        hi, lo = split(inv.reshape(64, 64))
        lyi[gy] = np.concatenate([hi, lo, hi], 1)

    ax = angles(np.arange(NX), kept(KX, NX), NX).reshape(16, 8, KX)
    c = np.broadcast_to(np.cos(ax).transpose(0, 2, 1)[:, :, None, :], (16, KX, 8, 8)).reshape(16, KX, 64)
    s = np.broadcast_to(np.sin(ax).transpose(0, 2, 1)[:, :, None, :], (16, KX, 8, 8)).reshape(16, KX, 64)
    tx = np.stack([np.concatenate([c, s], 2), np.concatenate([-s, c], 2)], 0)

    core, ri, ch, x = np.unravel_index(np.arange(256), (2, 2, 8, 8))
    o, i = np.unravel_index(np.arange(256), (16, 16))
    e1 = (i[None, :] == (core * 8 + ch)[:, None]).astype(np.float64)
    e2 = (o[:, None] == (core * 8 + ch)[None, :]).astype(np.float64)
    i128 = np.arange(128) // 8
    ecol = (np.arange(256)[:, None] % 16 == i128[None, :]).astype(np.float64)
    xo = np.arange(8)[:, None]
    xi = (np.arange(128) % 8)[None, :]
    mask = np.stack([(xi - xo == a - 1) for a in range(3)], 0).astype(np.float32)
    eh = np.zeros((2, 256, 128))
    mh = np.zeros((3, 8, 128), np.float32)
    for part, (hi_lo) in enumerate("hlh"):
        for side in range(2):
            lanes = part * 32 + side * 16 + np.arange(16)
            eh[0 if hi_lo == "h" else 1, np.arange(256), lanes[np.arange(256) % 16]] = 1.0
            mh[2 * side, 0 if side == 0 else 7, lanes] = 1.0
    return dict(
        tzf=bf(tzf), tzi=bf(tzi), lyf=bf(lyf), lyi=bf(lyi), tx=tx.astype(np.float32), e1=bf(e1), e2=bf(e2),
        ecol=bf(ecol), eh=bf(eh), mask=mask, mh=mh, eye=np.eye(32, 27, dtype=np.float32),
    )


TABLES = tables()
NAMES = ("tzf", "tzi", "lyf", "lyi", "tx", "e1", "e2", "ecol", "eh", "mask", "mh", "eye")


def hilo(v):
    hi = v.astype(BF16)
    return hi, (v - hi.astype(F32)).astype(BF16)


def mm(a, b, dims=(((1,), (0,)), ((), ()))):
    return lax.dot_general(a, b, dims, preferred_element_type=F32)


def erf(x):
    x = jnp.clip(x, -3.832506856900711, 3.832506856900711)
    t = x * x
    p = 0.00022905065861350646
    for coef in (0.0034082910107109506, 0.050955695062380861, 0.18520832239976145, 1.128379143519084):
        p = p * t + coef
    q = -1.1791602954361697e-7
    for coef in (0.000023547966471313185, 0.0010179625278914885, 0.014070470171167667, 0.11098505178285362,
                 0.49746925110067538, 1.0):
        q = q * t + coef
    return x * p / q


def gelu(v):
    return 0.5 * v * (1.0 + erf(v * 0.7071067811865476))


FAR_Z = (4, 3, 5, 2, 6, 1, 7, 0)
FAR_X = (2, 1, 3, 0)


def kernel(f2, f3, w_hbm, cw, tzf, tzi, lyf, lyi, tx, e1, e2, ecol, eh, mask, mh, eye, v_out, *refs):
    (fv, wv, cwv, tzf_v, tzi_v, tx_v, e1_v, e2_v, ecol_v, eh_v, mask_v, mh_v, eye_v, lyf_v, lyi_v,
     ws, wb, wg, b, lhs, xs, yh_s, yh, xh, cs, ch, za, zr, ps, pr, rs, rb, co_s, rc, g3, u, ur, co,
     ld, a_s, a_r, h_s, h_r, y_s, y_r, b_s, b_r, c_s, c_r, d_s, d_r, w_s, w_r, u_s, u_r) = refs
    gx = lax.axis_index("gx")
    gy = lax.axis_index("gy")
    y = gy // 4
    jj = gy % 4
    s = gy % 2
    x = gx % 4
    z = (gx // 4) + 4 * (jj // 2)
    me = jj * 16 + gx
    gxm, gxp = (gx + 15) % 16, (gx + 1) % 16
    gym, gyp = (gy + 15) % 16, (gy + 1) % 16

    far = pl.multiple_of((1 - s) * 1024, 1024)
    near = pl.multiple_of(s * 1024, 1024)
    loads = [(f2.at[pl.ds(far, 1024)], fv.at[pl.ds(far, 1024)]), (w_hbm, wv), (cw, cwv), (lyf.at[gy], lyf_v), (lyi.at[gy], lyi_v), (tzf, tzf_v), (tzi, tzi_v),
             (tx, tx_v), (e1, e1_v), (e2, e2_v), (ecol, ecol_v), (eh, eh_v), (mask, mask_v), (mh, mh_v), (eye, eye_v),
             (f2.at[pl.ds(near, 1024)], fv.at[pl.ds(near, 1024)])]
    copies = [pltpu.make_async_copy(src, dst, ld.at[n]) for n, (src, dst) in enumerate(loads)]
    for n in (0, 5, 15):
        copies[n].start()

    xs4 = [(x + dx) % 4 for dx in FAR_X]
    peers = []
    for dz in FAR_Z:
        zz = (z + dz) % 8
        base, hi2 = (zz % 4) * 4, (zz // 4) * 2
        for n, dx in enumerate(FAR_X):
            for dc in (1, 0):
                if dz or dx or dc:
                    peers.append((base + xs4[n], hi2 + (s + dc) % 2))

    partner = jj + 1 - 2 * s + 4 * y
    barrier = pltpu.get_barrier_semaphore()

    def greet(px, py):
        pl.semaphore_signal(barrier, inc=1, device_id=(px, py), device_id_type=MESH)

    for px in (gxm, gx, gxp):
        for py in (gym, gyp):
            greet(px, py)
    for px, pj in peers:
        greet(px, 4 * y + pj)
    for step in (2, 1, 3):
        greet(gx, (gy + 4 * step) % 16)
    for n in (3, 1, 14, 2, 10, 11, 12, 13, 7, 8, 9, 4, 6):
        copies[n].start()

    def part(h):
        r0 = pl.multiple_of(h * 64, 64)
        for yy in range(16):
            a = jnp.concatenate([fv[pl.ds(h * 1024 + c * 128 + yy, 8, stride=16), :] for c in range(8)], 0)
            hi, lo = hilo(a)
            lanes = slice((yy + 1) * 128, (yy + 2) * 128)
            b[pl.ds(r0, 64), lanes] = hi
            b[pl.ds(r0 + 128, 64), lanes] = lo
            b[pl.ds(r0 + 256, 64), lanes] = hi
            if yy in (0, 15):
                yh_s[0 if yy == 0 else 1, pl.ds(r0, 64), :] = a

    def along_z(h):
        r0 = pl.multiple_of(h * 64, 64)
        for yy in range(8):
            l0 = (2 * yy + 1) * 128
            hi = jnp.concatenate([b[pl.ds(r0, 64), l0:l0 + 128], b[pl.ds(r0, 64), l0 + 128:l0 + 256]], 0)
            lo = jnp.concatenate([b[pl.ds(r0 + 128, 64), l0:l0 + 128], b[pl.ds(r0 + 128, 64), l0 + 128:l0 + 256]], 0)
            r = mm(tzf_v[...], jnp.concatenate([hi, hi, lo], 1), (((1,), (1,)), ((), ())))
            za[h, pl.ds(yy, 24, stride=8), :] = r

    copies[0].wait()
    part(1 - s)
    copies[5].wait()
    along_z(1 - s)
    pl.semaphore_wait(barrier, 72)

    def remote(src, dst, ssem, rsem, px, py):
        return pltpu.make_async_remote_copy(src_ref=src, dst_ref=dst, send_sem=ssem, recv_sem=rsem,
                                            device_id=(px, py), device_id_type=MESH)

    acopies = [remote(za.at[1 - s, pl.ds(48 * n, 48)], zr.at[pl.ds(48 * n, 48)], a_s.at[n], a_r.at[n], gx, partner)
               for n in range(4)]
    for copy in acopies:
        copy.start()
    halos = [
        remote(f3.at[:, pl.ds(112, 16), :], xh.at[0], h_s.at[0], h_r.at[0], gxp, gy),
        remote(f3.at[:, pl.ds(0, 16), :], xh.at[1], h_s.at[1], h_r.at[1], gxm, gy),
        remote(yh_s.at[1], yh.at[0], h_s.at[2], h_r.at[2], gx, gyp),
        remote(yh_s.at[0], yh.at[1], h_s.at[3], h_r.at[3], gx, gym),
        remote(cs.at[0], ch.at[3], h_s.at[4], h_r.at[7], gxm, gym),
        remote(cs.at[1], ch.at[2], h_s.at[5], h_r.at[6], gxm, gyp),
        remote(cs.at[2], ch.at[1], h_s.at[6], h_r.at[5], gxp, gym),
        remote(cs.at[3], ch.at[0], h_s.at[7], h_r.at[4], gxp, gyp),
    ]
    for copy in halos[0:2]:
        copy.start()
    copies[15].wait()
    part(s)

    @pl.when(jj != 3)
    def _():
        halos[2].start()

    @pl.when(jj != 0)
    def _():
        halos[3].start()

    along_z(s)

    copies[1].wait()
    copies[14].wait()
    for n in range(4):
        t = lax.dot_general(eye_v[...], wv[pl.ds(128 * n, 128), :], (((1,), (1,)), ((), ())),
                            precision=lax.Precision.HIGHEST, preferred_element_type=F32)
        for m in range(27):
            ws[m, n, :] = t[m, :]

    odd = gx % 2 == 1

    def w_copy(m):
        picks = []
        for mode in (m, m + 27):
            l = mode % 18
            d = 8 * (l // 9) + max(l % 9 - 1, 0)
            picks.append((d, int(l % 9 == 1), mode // 18))
        dx, slot, p = (a if a == b else jnp.where(odd, b, a) for a, b in zip(*picks))
        p = 3 * (gx // 2) + p
        mine = dx == gx
        return mine, slot, p, remote(ws.at[m], wb.at[slot, p], w_s.at[m], w_r.at[slot], dx, gy)

    wcopies = [w_copy(m) for m in range(27)]
    for m, (mine, slot, p, copy) in enumerate(wcopies):
        @pl.when(jnp.logical_not(mine))
        def _():
            copy.start()

        @pl.when(mine)
        def _():
            pltpu.make_async_copy(ws.at[m], wb.at[slot, p], w_r.at[slot]).start()

    copies[3].wait()
    half = lax.broadcasted_iota(jnp.int32, (24, 128), 1) < 64
    for k in range(12):
        if k % 3 == 0:
            acopies[k // 3].wait_recv()
        v = jnp.concatenate([za[s, 16 * k:16 * k + 16, :], zr[16 * k:16 * k + 16, :]], 0)
        hi, lo = hilo(v)
        r = mm(lyf_v[...], jnp.concatenate([hi, hi, lo], 0))
        p0 = jnp.where(half, r[0:24], r[72:96])
        p1 = jnp.where(half, r[24:48], r[48:72])
        ps[pl.ds(k, 24, stride=12), :] = p0 + pltpu.roll(p1, 64, 1)

    ycopies = []
    for step in (2, 1, 3):
        yt = (y + step) % 4
        copy = remote(ps.at[pl.ds(pl.multiple_of(yt * 72, 8), 72), :], pr.at[step - 1], y_s.at[step - 1],
                      y_r.at[step - 1], gx, yt * 4 + jj)
        copy.start()
        ycopies.append(copy)

    @pl.when(jj == 3)
    def _():
        halos[2].start()

    @pl.when(jj == 0)
    def _():
        halos[3].start()

    for n, (x0, y0) in enumerate(((0, 0), (0, 15), (7, 0), (7, 15))):
        cs[n] = jnp.concatenate([fv[pl.ds(c * 128 + x0 * 16 + y0, 1), :] for c in range(16)], 0)
    rs[72] = jnp.zeros((1, 128), F32)
    for copy in halos[4:]:
        copy.start()


    for copy in ycopies:
        copy.wait_recv()
    total = ps[pl.ds(pl.multiple_of(y * 72, 8), 72), :] + pr[0] + pr[1] + pr[2]
    for r in range(72):
        rs[r, :, :] = total[r:r + 1, :]

    def b_copy(px, pj):
        d = pj * 16 + px
        u8 = d % 8
        r = 9 * (d // 8) + u8 + (u8 > 0).astype(jnp.int32)
        return rs.at[pl.ds(r, 2)], px, 4 * y + pj

    for px, pj in peers:
        src, dx, dy = b_copy(px, pj)
        remote(src, rb.at[me], b_s, b_r, dx, dy).start()
    src, _, _ = b_copy(gx, jj)
    pltpu.make_async_copy(src, rb.at[me], b_r).start()
    double = me % 8 == 0

    for n in (2, 10, 11, 12, 13):
        copies[n].wait()
    cwt = lax.dot_general(eye_v[...], cwv[...], (((1,), (1,)), ((), ())),
                          precision=lax.Precision.HIGHEST, preferred_element_type=F32)
    group = lax.broadcasted_iota(jnp.int32, (32, 256), 1) // 16
    picked = jnp.concatenate([jnp.where(group == o, cwt, 0.0) for o in range(16)], 0)
    whi, wlo = hilo(picked)
    xs[0] = mm(whi, ecol_v[...])
    xs[1] = mm(wlo, ecol_v[...])
    xs[2] = mm(whi, eh_v[0]) + mm(wlo, eh_v[1])

    def spread(op, carry):
        for t in range(3):
            ms = [mask_v[a] > 0 if t < 2 else mh_v[a] > 0 for a in range(3)]
            for yb in range(3):
                parts = []
                for oo in range(2):
                    for zc in range(3):
                        v = jnp.zeros((8, 128), F32)
                        for a in range(3) if t < 2 else (0, 2):
                            row = xs[t, pl.ds((2 * op + oo) * 32 + 9 * a + 3 * yb + zc, 1), :]
                            v = jnp.where(ms[a], jnp.broadcast_to(row, (8, 128)), v)
                        parts.append(v)
                v = jnp.concatenate(parts, 0).astype(BF16)
                rows = pl.ds(pl.multiple_of(384 * yb + 48 * op, 16), 48)
                if t == 0:
                    lhs[rows, 0:128] = v
                    lhs[rows, 128:256] = v
                else:
                    lhs[rows, 128 + 128 * t:256 + 128 * t] = v
        return carry

    lax.fori_loop(0, 8, spread, 0)

    def conv(pair, carry):
        acc = jnp.zeros((384, 256), F32)
        for t in range(3):
            lanes = pl.ds(pl.multiple_of((2 * pair + t) * 128, 128), 256)
            acc = acc + mm(lhs[384 * t:384 * t + 384, :], b[:, lanes])
        for n in range(2):
            v = acc[:, 128 * n:128 * n + 128].reshape(16, 3, 8, 128)
            v0, v1, v2 = (v[:, i].reshape(128, 128) for i in range(3))
            v = v1 + pltpu.roll(v0, 1, 1) + pltpu.roll(v2, 127, 1)
            co[pl.ds(pl.multiple_of((2 * pair + n) * 128, 128), 128), :] = v
        return carry

    for n in (7, 8, 9):
        copies[n].wait()
    def gather(slot):
        pltpu.make_async_copy(wb.at[slot], wb.at[slot], w_r.at[slot]).wait()
        for t in range(4):
            for p in range(24):
                wg[slot, t // 2, p:p + 1, 128 * (t % 2):128 * (t % 2) + 128] = wb[slot, p, t:t + 1, :]

    gather(0)

    @pl.when(double)
    def _():
        gather(1)

    pltpu.make_async_copy(rb, rb, b_r).wait()

    def mix(slots):
        accs = [[[jnp.zeros((24, 128), F32) for _ in range(2)] for _ in range(2)] for _ in slots]
        for g in range(16):
            for core in range(2):
                for n, slot in enumerate(slots):
                    row = rb[16 * core + g, slot] + rb[16 * core + 32 + g, slot]
                    row = jnp.broadcast_to(row, (24, 128))
                    for part in range(2):
                        accs[n][part][core] = accs[n][part][core] + tx_v[part, g] * row
        acc = jnp.concatenate([jnp.concatenate(accs[n][part], 1) for n in range(len(slots)) for part in range(2)], 0)
        size = 48 * len(slots)
        hi, lo = hilo(acc)
        cc = mm(jnp.concatenate([hi, lo], 0), e1_v[...])
        cc = cc[0:size] + cc[size:2 * size]
        prods = []
        for n, slot in enumerate(slots):
            cr, ci = cc[48 * n:48 * n + 24], cc[48 * n + 24:48 * n + 48]
            wr, wi = wg[slot, 0], wg[slot, 1]
            prods += [wr * cr - wi * ci, wr * ci + wi * cr]
        hi, lo = hilo(jnp.concatenate(prods, 0))
        mx = mm(jnp.concatenate([hi, lo], 0), e2_v[...])
        mx = mx[0:size] + mx[size:2 * size]
        for g in range(16):
            for core in range(2):
                for n, slot in enumerate(slots):
                    lanes = slice(128 * core, 128 * core + 128)
                    row = tx_v[0, g] * mx[48 * n:48 * n + 24, lanes] + tx_v[1, g] * mx[48 * n + 24:48 * n + 48, lanes]
                    co_s[2 * g + core, slot] = jnp.sum(row, axis=0, keepdims=True)
                if len(slots) == 1:
                    co_s[2 * g + core, 1] = jnp.zeros((1, 128), F32)

    @pl.when(double)
    def _():
        mix((0, 1))

    @pl.when(jnp.logical_not(double))
    def _():
        mix((0,))

    for px, pj in peers:
        remote(co_s.at[2 * px + pj % 2], rc.at[me], c_s, c_r, px, 4 * y + pj).start()
    pltpu.make_async_copy(co_s.at[2 * gx + s], rc.at[me], c_r).start()

    b[384:512, :] = jnp.zeros((128, 18 * 128), BF16)
    for copy in halos:
        copy.wait_recv()
    for yi, side in ((0, 0), (17, 1)):
        hi, lo = hilo(yh[side])
        lanes = slice(yi * 128, yi * 128 + 128)
        b[0:128, lanes] = hi
        b[128:256, lanes] = lo
        b[256:384, lanes] = hi
    for yi in range(18):
        if yi == 0:
            v = jnp.concatenate([ch[0], ch[2]], 0)
        elif yi == 17:
            v = jnp.concatenate([ch[1], ch[3]], 0)
        else:
            v = jnp.concatenate([xh[side, c, pl.ds(yi - 1, 1), :] for side in range(2) for c in range(16)], 0)
        hi, lo = hilo(v)
        b[384:480, yi * 128:yi * 128 + 128] = jnp.concatenate([hi, hi, lo], 0)

    lax.fori_loop(0, 8, conv, 0)

    for t in range(4):
        g3[t, 72:96, :] = jnp.zeros((24, 128), F32)
    pltpu.make_async_copy(rc, rc, c_r).wait()
    for r in range(72):
        t8, u8 = r // 9, r % 9
        g3[0, r:r + 1, :] = rc[8 * t8 + max(u8 - 1, 0), 1 if u8 == 1 else 0]
    dcopies = []
    for step in (2, 1, 3):
        yt = (y + step) % 4
        copy = remote(g3.at[0, pl.ds(0, 72)], g3.at[4 - step, pl.ds(0, 72)], d_s.at[step - 1], d_r.at[4 - step],
                      gx, yt * 4 + jj)
        copy.start()
        dcopies.append(copy)
    copies[4].wait()
    copies[6].wait()
    for copy in dcopies:
        copy.wait_recv()

    ucopies = [remote(u.at[1, pl.ds(48 * n, 48)], ur.at[pl.ds(48 * n, 48)], u_s.at[n], u_r.at[n], gx, partner)
               for n in range(4)]
    half16 = lax.broadcasted_iota(jnp.int32, (16, 128), 1) < 64
    for k in range(12):
        v = jnp.concatenate([g3[(t - y + 4) % 4, pl.ds(k, 8, stride=12), :] for t in range(4)], 0)
        v = jnp.concatenate([v, pltpu.roll(v, 64, 1)], 0)
        hi, lo = hilo(v)
        r = mm(lyi_v[...], jnp.concatenate([hi, hi, lo], 0))
        for part in range(2):
            v = jnp.where(half16, r[16 * part:16 * part + 16], r[32 + 16 * part:48 + 16 * part])
            for dst in range(2):
                u[dst, 16 * k + 8 * part:16 * k + 8 * part + 8, :] = v[8 * dst:8 * dst + 8]
        if k % 3 == 2:
            ucopies[k // 3].start()

    zero8 = jnp.zeros((8, 128), F32)

    def finish(v, hh, yy, act):
        hi, lo = hilo(jnp.concatenate([v, zero8], 0))
        r = mm(jnp.concatenate([hi, hi, lo], 0), tzi_v[...], (((0,), (0,)), ((), ())))
        for yp in range(2):
            yr = 2 * yy + yp
            t = r[64 * yp:64 * yp + 64] + co[pl.ds(pl.multiple_of(yr * 128 + hh * 64, 64), 64), :]
            t = gelu(t) if act else t
            for c in range(8):
                v_out[pl.ds(hh * 1024 + c * 128 + yr, 8, stride=16), :] = t[8 * c:8 * c + 8]

    for yy in range(8):
        finish(u[0, pl.ds(yy, 24, stride=8), :], s, yy, True)
    for copy in ucopies:
        copy.wait_recv()
    for yy in range(8):
        finish(ur[pl.ds(yy, 24, stride=8), :], 1 - s, yy, False)

    for copy in acopies + ucopies + halos + ycopies + dcopies:
        copy.wait_send()

    for mine, slot, p, copy in wcopies:
        @pl.when(jnp.logical_not(mine))
        def _():
            copy.wait_send()

    part = rb.at[pl.ds(0, 63)]
    pltpu.make_async_copy(part, part, b_s).wait()
    pltpu.make_async_copy(part, part, c_s).wait()


def gelu_kernel(v, out_hbm, outv, sem):
    s = lax.axis_index("gy") % 2
    ready = pl.ds(pl.multiple_of(s * 1024, 1024), 1024)
    copies = [pltpu.make_async_copy(v.at[ready], out_hbm.at[ready], sem.at[4])]
    copies[0].start()
    for n in range(4):
        start = pl.multiple_of((1 - s) * 1024 + 256 * n, 256)
        for m in range(4):
            outv[pl.ds(256 * n + 64 * m, 64), :] = gelu(v[pl.ds(start + 64 * m, 64), :])
        copy = pltpu.make_async_copy(outv.at[pl.ds(256 * n, 256)], out_hbm.at[pl.ds(start, 256)], sem.at[n])
        copy.start()
        copies.append(copy)
    for copy in copies:
        copy.wait()


def shards(features, conv_weight, mix_weight):
    f2 = features.reshape(2048, 128)
    f3 = features.reshape(16, 128, 128)
    w = mix_weight.reshape(512, 27)
    cw = conv_weight.transpose(1, 2, 0).reshape(256, 27)
    consts = [jnp.asarray(TABLES[n]) for n in NAMES]
    vm = pltpu.VMEM
    dma = pltpu.SemaphoreType.DMA
    scratch = [
        vm((2048, 128), F32), vm((512, 27), F32), vm((256, 27), F32),
        vm((24, 384), BF16), vm((96, 128), BF16), vm((2, 16, 24, 128), F32), vm((256, 256), BF16), vm((256, 256), BF16),
        vm((256, 128), BF16), vm((2, 256, 128), BF16), vm((3, 8, 128), F32), vm((3, 8, 128), F32), vm((32, 27), F32),
        vm((96, 96), BF16), vm((64, 192), BF16),
        vm((27, 4, 128), F32), vm((2, 24, 4, 128), F32), vm((2, 2, 24, 256), F32), vm((512, 18 * 128), BF16), vm((1152, 512), BF16),
        vm((3, 512, 128), F32),
        vm((2, 128, 128), F32), vm((2, 128, 128), F32), vm((2, 16, 16, 128), F32), vm((4, 16, 128), F32),
        vm((4, 16, 128), F32), vm((2, 192, 128), F32), vm((192, 128), F32), vm((288, 128), F32), vm((3, 72, 128), F32),
        vm((73, 1, 128), F32), vm((64, 2, 1, 128), F32), vm((32, 2, 1, 128), F32), vm((64, 2, 1, 128), F32),
        vm((4, 96, 128), F32), vm((2, 192, 128), F32), vm((192, 128), F32), vm((2048, 128), F32),
        dma((16,)), dma((4,)), dma((4,)), dma((8,)), dma((8,)), dma((3,)), dma((3,)), dma, dma, dma, dma,
        dma((3,)), dma((4,)), dma((27,)), dma((2,)), dma((4,)), dma((4,)),
    ]
    any_spec = pl.BlockSpec(memory_space=pl.ANY)
    vmem_spec = pl.BlockSpec(memory_space=pltpu.VMEM)
    hbm_spec = pl.BlockSpec(memory_space=pltpu.HBM)
    v = pl.pallas_call(
        kernel,
        out_shape=jax.ShapeDtypeStruct((2048, 128), F32),
        in_specs=[hbm_spec] * (4 + len(NAMES)),
        out_specs=vmem_spec,
        scratch_shapes=scratch,
        compiler_params=pltpu.CompilerParams(collective_id=0, has_side_effects=True,
                                             vmem_limit_bytes=40 * 1024 * 1024),
        name="layer",
    )(*[pltpu.with_memory_space_constraint(a, pltpu.HBM) for a in (f2, f3, w, cw, *consts)])
    out = pl.pallas_call(
        gelu_kernel,
        out_shape=jax.ShapeDtypeStruct((2048, 128), F32),
        in_specs=[vmem_spec],
        out_specs=any_spec,
        scratch_shapes=[vm((1024, 128), F32), dma((5,))],
        compiler_params=pltpu.CompilerParams(vmem_limit_bytes=8 * 1024 * 1024),
        name="act",
    )(v)
    return out.reshape(features.shape)


def solution(mesh):
    in_specs = (P(None, "gx", "gy", None), P(), P(None, None, None, "gy", "gx"))
    return jax.shard_map(shards, mesh=mesh, in_specs=in_specs, out_specs=P(None, "gx", "gy", None), check_vma=False)
```

```python
import functools
import math

import jax
import jax.numpy as jnp
import numpy as np
from jax import lax
from jax.experimental import pallas as pl
from jax.experimental.pallas import tpu as pltpu
from jax.sharding import PartitionSpec as P

C, NX, NY, NZ = 16, 128, 256, 128
KX, KY, KZ = 24, 24, 12
F32, BF16 = jnp.float32, jnp.bfloat16
MESH = pl.DeviceIdType.MESH


def split(a):
    hi = round_bf16(a)
    return hi, round_bf16(np.asarray(a, np.float64) - hi)


def round_bf16(a):
    import ml_dtypes

    return np.asarray(a, np.float32).astype(ml_dtypes.bfloat16).astype(np.float64)


def bf(a):
    import ml_dtypes

    return np.asarray(a, np.float32).astype(ml_dtypes.bfloat16)


def angles(positions, frequencies, length):
    return 2.0 * math.pi * ((positions[:, None] * frequencies[None, :]) % length) / length


def kept(amount, length):
    index = np.arange(amount)
    return np.where(index < amount // 2, index, length - amount + index)


def tables():
    forward = 1.0 / math.sqrt(NX * NY * NZ)
    inverse = 1.0 / math.sqrt(KX * KY * KZ)
    az = angles(np.arange(NZ), np.arange(KZ), NZ).T
    tz = np.stack([np.cos(az), -np.sin(az)], 1).reshape(2 * KZ, NZ)
    hi, lo = split(tz * forward)
    tzf = np.concatenate([hi, lo, hi], 1)
    pad = np.zeros((8, NZ))
    hi, lo = split(np.concatenate([tz * inverse, pad], 0))
    tzi = np.concatenate([hi, lo, hi], 0)

    qs = kept(KY, NY)
    lyf = np.zeros((16, 96, 96))
    lyi = np.zeros((16, 64, 192))
    for gy in range(16):
        fwd = np.zeros((2, 2, KY, 2, 2, 8))
        inv = np.zeros((2, 2, 2, 8, 2, KY))
        for own in range(2):
            start = 16 * (gy if own == 0 else gy ^ 1)
            for yp in range(2):
                a = angles(start + 2 * np.arange(8) + yp, qs, NY)
                c, s = np.cos(a), np.sin(a)
                fwd[yp, 0, :, own, 0] = c.T
                fwd[yp, 0, :, own, 1] = s.T
                fwd[yp, 1, :, own, 0] = -s.T
                fwd[yp, 1, :, own, 1] = c.T
                re = (c, -s)
                im = (s, c)
                for v in range(2):
                    w = v if yp == 0 else 1 - v
                    inv[yp, 0, own, :, v] = re[w]
                    inv[yp, 1, own, :, v] = im[w]
        hi, lo = split(fwd.reshape(96, 32))
        lyf[gy] = np.concatenate([hi, lo, hi], 1)
        inv = np.concatenate([inv.reshape(64, 2, 4, 6), np.zeros((64, 2, 4, 2))], 3)
        hi, lo = split(inv.reshape(64, 64))
        lyi[gy] = np.concatenate([hi, lo, hi], 1)

    ax = angles(np.arange(NX), kept(KX, NX), NX).reshape(16, 8, KX)
    c = np.broadcast_to(np.cos(ax).transpose(0, 2, 1)[:, :, None, :], (16, KX, 8, 8)).reshape(16, KX, 64)
    s = np.broadcast_to(np.sin(ax).transpose(0, 2, 1)[:, :, None, :], (16, KX, 8, 8)).reshape(16, KX, 64)
    tx = np.stack([np.concatenate([c, s], 2), np.concatenate([-s, c], 2)], 0)

    core, ri, ch, x = np.unravel_index(np.arange(256), (2, 2, 8, 8))
    o, i = np.unravel_index(np.arange(256), (16, 16))
    e1 = (i[None, :] == (core * 8 + ch)[:, None]).astype(np.float64)
    e2 = (o[:, None] == (core * 8 + ch)[None, :]).astype(np.float64)
    i128 = np.arange(128) // 8
    ecol = (np.arange(256)[:, None] % 16 == i128[None, :]).astype(np.float64)
    xo = np.arange(8)[:, None]
    xi = (np.arange(128) % 8)[None, :]
    mask = np.stack([(xi - xo == a - 1) for a in range(3)], 0).astype(np.float32)
    eh = np.zeros((2, 256, 128))
    mh = np.zeros((3, 8, 128), np.float32)
    for part, (hi_lo) in enumerate("hlh"):
        for side in range(2):
            lanes = part * 32 + side * 16 + np.arange(16)
            eh[0 if hi_lo == "h" else 1, np.arange(256), lanes[np.arange(256) % 16]] = 1.0
            mh[2 * side, 0 if side == 0 else 7, lanes] = 1.0
    return dict(
        tzf=bf(tzf), tzi=bf(tzi), lyf=bf(lyf), lyi=bf(lyi), tx=tx.astype(np.float32), e1=bf(e1), e2=bf(e2),
        ecol=bf(ecol), eh=bf(eh), mask=mask, mh=mh, eye=np.eye(32, 27, dtype=np.float32),
    )


TABLES = tables()
NAMES = ("tzf", "tzi", "lyf", "lyi", "tx", "e1", "e2", "ecol", "eh", "mask", "mh", "eye")


def hilo(v):
    hi = v.astype(BF16)
    return hi, (v - hi.astype(F32)).astype(BF16)


def mm(a, b, dims=(((1,), (0,)), ((), ()))):
    return lax.dot_general(a, b, dims, preferred_element_type=F32)


def erf(x):
    x = jnp.clip(x, -3.832506856900711, 3.832506856900711)
    t = x * x
    p = 0.00022905065861350646
    for coef in (0.0034082910107109506, 0.050955695062380861, 0.18520832239976145, 1.128379143519084):
        p = p * t + coef
    q = -1.1791602954361697e-7
    for coef in (0.000023547966471313185, 0.0010179625278914885, 0.014070470171167667, 0.11098505178285362,
                 0.49746925110067538, 1.0):
        q = q * t + coef
    return x * p / q


def gelu(v):
    return 0.5 * v * (1.0 + erf(v * 0.7071067811865476))


FAR_Z = (4, 3, 5, 2, 6, 1, 7, 0)
FAR_X = (2, 1, 3, 0)


def kernel(f2, f3, w_hbm, cw, tzf, tzi, lyf, lyi, tx, e1, e2, ecol, eh, mask, mh, eye, v_out, *refs):
    (fv, wv, cwv, tzf_v, tzi_v, tx_v, e1_v, e2_v, ecol_v, eh_v, mask_v, mh_v, eye_v, lyf_v, lyi_v,
     ws, wb, wg, b, lhs, xs, yh_s, yh, xh, cs, ch, za, zr, ps, pr, rs, rb, co_s, rc, g3, u, ur, co,
     ld, a_s, a_r, h_s, h_r, y_s, y_r, b_s, b_r, c_s, c_r, d_s, d_r, w_s, w_r, u_s, u_r) = refs
    gx = lax.axis_index("gx")
    gy = lax.axis_index("gy")
    y = gy // 4
    jj = gy % 4
    s = gy % 2
    x = gx % 4
    z = (gx // 4) + 4 * (jj // 2)
    me = jj * 16 + gx
    gxm, gxp = (gx + 15) % 16, (gx + 1) % 16
    gym, gyp = (gy + 15) % 16, (gy + 1) % 16

    far = pl.multiple_of((1 - s) * 1024, 1024)
    near = pl.multiple_of(s * 1024, 1024)
    loads = [(f2.at[pl.ds(far, 1024)], fv.at[pl.ds(far, 1024)]), (w_hbm, wv), (cw, cwv), (lyf.at[gy], lyf_v), (lyi.at[gy], lyi_v), (tzf, tzf_v), (tzi, tzi_v),
             (tx, tx_v), (e1, e1_v), (e2, e2_v), (ecol, ecol_v), (eh, eh_v), (mask, mask_v), (mh, mh_v), (eye, eye_v),
             (f2.at[pl.ds(near, 1024)], fv.at[pl.ds(near, 1024)])]
    copies = [pltpu.make_async_copy(src, dst, ld.at[n]) for n, (src, dst) in enumerate(loads)]
    for n in (0, 5, 15):
        copies[n].start()

    xs4 = [(x + dx) % 4 for dx in FAR_X]
    peers = []
    for dz in FAR_Z:
        zz = (z + dz) % 8
        base, hi2 = (zz % 4) * 4, (zz // 4) * 2
        for n, dx in enumerate(FAR_X):
            for dc in (1, 0):
                if dz or dx or dc:
                    peers.append((base + xs4[n], hi2 + (s + dc) % 2))

    partner = jj + 1 - 2 * s + 4 * y
    barrier = pltpu.get_barrier_semaphore()

    def greet(px, py):
        pl.semaphore_signal(barrier, inc=1, device_id=(px, py), device_id_type=MESH)

    for px in (gxm, gx, gxp):
        for py in (gym, gyp):
            greet(px, py)
    for px, pj in peers:
        greet(px, 4 * y + pj)
    for step in (2, 1, 3):
        greet(gx, (gy + 4 * step) % 16)
    for n in (3, 1, 14, 2, 10, 11, 12, 13, 7, 8, 9, 4, 6):
        copies[n].start()

    def part(h):
        r0 = pl.multiple_of(h * 64, 64)
        for yy in range(16):
            a = jnp.concatenate([fv[pl.ds(h * 1024 + c * 128 + yy, 8, stride=16), :] for c in range(8)], 0)
            hi, lo = hilo(a)
            lanes = slice((yy + 1) * 128, (yy + 2) * 128)
            b[pl.ds(r0, 64), lanes] = hi
            b[pl.ds(r0 + 128, 64), lanes] = lo
            b[pl.ds(r0 + 256, 64), lanes] = hi
            if yy in (0, 15):
                yh_s[0 if yy == 0 else 1, pl.ds(r0, 64), :] = a

    def along_z(h):
        r0 = pl.multiple_of(h * 64, 64)
        for yy in range(8):
            l0 = (2 * yy + 1) * 128
            hi = jnp.concatenate([b[pl.ds(r0, 64), l0:l0 + 128], b[pl.ds(r0, 64), l0 + 128:l0 + 256]], 0)
            lo = jnp.concatenate([b[pl.ds(r0 + 128, 64), l0:l0 + 128], b[pl.ds(r0 + 128, 64), l0 + 128:l0 + 256]], 0)
            r = mm(tzf_v[...], jnp.concatenate([hi, hi, lo], 1), (((1,), (1,)), ((), ())))
            za[h, pl.ds(yy, 24, stride=8), :] = r

    copies[0].wait()
    part(1 - s)
    copies[5].wait()
    along_z(1 - s)
    pl.semaphore_wait(barrier, 72)

    def remote(src, dst, ssem, rsem, px, py):
        return pltpu.make_async_remote_copy(src_ref=src, dst_ref=dst, send_sem=ssem, recv_sem=rsem,
                                            device_id=(px, py), device_id_type=MESH)

    acopies = [remote(za.at[1 - s, pl.ds(48 * n, 48)], zr.at[pl.ds(48 * n, 48)], a_s.at[n], a_r.at[n], gx, partner)
               for n in range(4)]
    for copy in acopies:
        copy.start()
    halos = [
        remote(f3.at[:, pl.ds(112, 16), :], xh.at[0], h_s.at[0], h_r.at[0], gxp, gy),
        remote(f3.at[:, pl.ds(0, 16), :], xh.at[1], h_s.at[1], h_r.at[1], gxm, gy),
        remote(yh_s.at[1], yh.at[0], h_s.at[2], h_r.at[2], gx, gyp),
        remote(yh_s.at[0], yh.at[1], h_s.at[3], h_r.at[3], gx, gym),
        remote(cs.at[0], ch.at[3], h_s.at[4], h_r.at[7], gxm, gym),
        remote(cs.at[1], ch.at[2], h_s.at[5], h_r.at[6], gxm, gyp),
        remote(cs.at[2], ch.at[1], h_s.at[6], h_r.at[5], gxp, gym),
        remote(cs.at[3], ch.at[0], h_s.at[7], h_r.at[4], gxp, gyp),
    ]
    for copy in halos[0:2]:
        copy.start()
    copies[15].wait()
    part(s)

    for n, (x0, y0) in enumerate(((0, 0), (0, 15), (7, 0), (7, 15))):
        cs[n] = jnp.concatenate([fv[pl.ds(c * 128 + x0 * 16 + y0, 1), :] for c in range(16)], 0)
    @pl.when(jj != 3)
    def _():
        halos[2].start()

    @pl.when(jj != 0)
    def _():
        halos[3].start()

    along_z(s)

    copies[1].wait()
    copies[14].wait()
    for n in range(4):
        t = lax.dot_general(eye_v[...], wv[pl.ds(128 * n, 128), :], (((1,), (1,)), ((), ())),
                            precision=lax.Precision.HIGHEST, preferred_element_type=F32)
        for m in range(27):
            ws[m, n, :] = t[m, :]

    odd = gx % 2 == 1

    def w_copy(m):
        picks = []
        for mode in (m, m + 27):
            l = mode % 18
            d = 8 * (l // 9) + max(l % 9 - 1, 0)
            picks.append((d, int(l % 9 == 1), mode // 18))
        dx, slot, p = (a if a == b else jnp.where(odd, b, a) for a, b in zip(*picks))
        p = 3 * (gx // 2) + p
        mine = dx == gx
        return mine, slot, p, remote(ws.at[m], wb.at[slot, p], w_s.at[m], w_r.at[slot], dx, gy)

    wcopies = [w_copy(m) for m in range(27)]
    for m, (mine, slot, p, copy) in enumerate(wcopies):
        @pl.when(jnp.logical_not(mine))
        def _():
            copy.start()

        @pl.when(mine)
        def _():
            pltpu.make_async_copy(ws.at[m], wb.at[slot, p], w_r.at[slot]).start()

    copies[3].wait()
    half = lax.broadcasted_iota(jnp.int32, (24, 128), 1) < 64
    for k in range(12):
        if k % 3 == 0:
            acopies[k // 3].wait_recv()
        v = jnp.concatenate([za[s, 16 * k:16 * k + 16, :], zr[16 * k:16 * k + 16, :]], 0)
        hi, lo = hilo(v)
        r = mm(lyf_v[...], jnp.concatenate([hi, hi, lo], 0))
        p0 = jnp.where(half, r[0:24], r[72:96])
        p1 = jnp.where(half, r[24:48], r[48:72])
        ps[pl.ds(k, 24, stride=12), :] = p0 + pltpu.roll(p1, 64, 1)

    ycopies = []
    for step in (2, 1, 3):
        yt = (y + step) % 4
        copy = remote(ps.at[pl.ds(pl.multiple_of(yt * 72, 8), 72), :], pr.at[step - 1], y_s.at[step - 1],
                      y_r.at[step - 1], gx, yt * 4 + jj)
        copy.start()
        ycopies.append(copy)

    rs[72] = jnp.zeros((1, 128), F32)


    for copy in ycopies:
        copy.wait_recv()
    total = ps[pl.ds(pl.multiple_of(y * 72, 8), 72), :] + pr[0] + pr[1] + pr[2]
    for r in range(72):
        rs[r, :, :] = total[r:r + 1, :]

    def b_copy(px, pj):
        d = pj * 16 + px
        u8 = d % 8
        r = 9 * (d // 8) + u8 + (u8 > 0).astype(jnp.int32)
        return rs.at[pl.ds(r, 2)], px, 4 * y + pj

    for px, pj in peers:
        src, dx, dy = b_copy(px, pj)
        remote(src, rb.at[me], b_s, b_r, dx, dy).start()
    src, _, _ = b_copy(gx, jj)
    pltpu.make_async_copy(src, rb.at[me], b_r).start()
    double = me % 8 == 0

    @pl.when(jj == 3)
    def _():
        halos[2].start()

    @pl.when(jj == 0)
    def _():
        halos[3].start()

    for copy in halos[4:]:
        copy.start()

    for n in (2, 10, 11, 12, 13):
        copies[n].wait()
    cwt = lax.dot_general(eye_v[...], cwv[...], (((1,), (1,)), ((), ())),
                          precision=lax.Precision.HIGHEST, preferred_element_type=F32)
    group = lax.broadcasted_iota(jnp.int32, (32, 256), 1) // 16
    picked = jnp.concatenate([jnp.where(group == o, cwt, 0.0) for o in range(16)], 0)
    whi, wlo = hilo(picked)
    xs[0] = mm(whi, ecol_v[...])
    xs[1] = mm(wlo, ecol_v[...])
    xs[2] = mm(whi, eh_v[0]) + mm(wlo, eh_v[1])

    def spread(op, carry):
        for t in range(3):
            ms = [mask_v[a] > 0 if t < 2 else mh_v[a] > 0 for a in range(3)]
            for yb in range(3):
                parts = []
                for oo in range(2):
                    for zc in range(3):
                        v = jnp.zeros((8, 128), F32)
                        for a in range(3) if t < 2 else (0, 2):
                            row = xs[t, pl.ds((2 * op + oo) * 32 + 9 * a + 3 * yb + zc, 1), :]
                            v = jnp.where(ms[a], jnp.broadcast_to(row, (8, 128)), v)
                        parts.append(v)
                v = jnp.concatenate(parts, 0).astype(BF16)
                rows = pl.ds(pl.multiple_of(384 * yb + 48 * op, 16), 48)
                if t == 0:
                    lhs[rows, 0:128] = v
                    lhs[rows, 128:256] = v
                else:
                    lhs[rows, 128 + 128 * t:256 + 128 * t] = v
        return carry

    lax.fori_loop(0, 8, spread, 0)

    def conv(pair, carry):
        acc = jnp.zeros((384, 256), F32)
        for t in range(3):
            lanes = pl.ds(pl.multiple_of((2 * pair + t) * 128, 128), 256)
            acc = acc + mm(lhs[384 * t:384 * t + 384, :], b[:, lanes])
        for n in range(2):
            v = acc[:, 128 * n:128 * n + 128].reshape(16, 3, 8, 128)
            v0, v1, v2 = (v[:, i].reshape(128, 128) for i in range(3))
            v = v1 + pltpu.roll(v0, 1, 1) + pltpu.roll(v2, 127, 1)
            co[pl.ds(pl.multiple_of((2 * pair + n) * 128, 128), 128), :] = v
        return carry

    for n in (7, 8, 9):
        copies[n].wait()
    def gather(slot):
        pltpu.make_async_copy(wb.at[slot], wb.at[slot], w_r.at[slot]).wait()
        for t in range(4):
            for p in range(24):
                wg[slot, t // 2, p:p + 1, 128 * (t % 2):128 * (t % 2) + 128] = wb[slot, p, t:t + 1, :]

    gather(0)

    @pl.when(double)
    def _():
        gather(1)

    pltpu.make_async_copy(rb, rb, b_r).wait()

    def mix(slots):
        accs = [[[jnp.zeros((24, 128), F32) for _ in range(2)] for _ in range(2)] for _ in slots]
        for g in range(16):
            for core in range(2):
                for n, slot in enumerate(slots):
                    row = rb[16 * core + g, slot] + rb[16 * core + 32 + g, slot]
                    row = jnp.broadcast_to(row, (24, 128))
                    for part in range(2):
                        accs[n][part][core] = accs[n][part][core] + tx_v[part, g] * row
        acc = jnp.concatenate([jnp.concatenate(accs[n][part], 1) for n in range(len(slots)) for part in range(2)], 0)
        size = 48 * len(slots)
        hi, lo = hilo(acc)
        cc = mm(jnp.concatenate([hi, lo], 0), e1_v[...])
        cc = cc[0:size] + cc[size:2 * size]
        prods = []
        for n, slot in enumerate(slots):
            cr, ci = cc[48 * n:48 * n + 24], cc[48 * n + 24:48 * n + 48]
            wr, wi = wg[slot, 0], wg[slot, 1]
            prods += [wr * cr - wi * ci, wr * ci + wi * cr]
        hi, lo = hilo(jnp.concatenate(prods, 0))
        mx = mm(jnp.concatenate([hi, lo], 0), e2_v[...])
        mx = mx[0:size] + mx[size:2 * size]
        for g in range(16):
            for core in range(2):
                for n, slot in enumerate(slots):
                    lanes = slice(128 * core, 128 * core + 128)
                    row = tx_v[0, g] * mx[48 * n:48 * n + 24, lanes] + tx_v[1, g] * mx[48 * n + 24:48 * n + 48, lanes]
                    co_s[2 * g + core, slot] = jnp.sum(row, axis=0, keepdims=True)
                if len(slots) == 1:
                    co_s[2 * g + core, 1] = jnp.zeros((1, 128), F32)

    @pl.when(double)
    def _():
        mix((0, 1))

    @pl.when(jnp.logical_not(double))
    def _():
        mix((0,))

    for px, pj in peers:
        remote(co_s.at[2 * px + pj % 2], rc.at[me], c_s, c_r, px, 4 * y + pj).start()
    pltpu.make_async_copy(co_s.at[2 * gx + s], rc.at[me], c_r).start()

    b[384:512, :] = jnp.zeros((128, 18 * 128), BF16)
    for copy in halos:
        copy.wait_recv()
    for yi, side in ((0, 0), (17, 1)):
        hi, lo = hilo(yh[side])
        lanes = slice(yi * 128, yi * 128 + 128)
        b[0:128, lanes] = hi
        b[128:256, lanes] = lo
        b[256:384, lanes] = hi
    for yi in range(18):
        if yi == 0:
            v = jnp.concatenate([ch[0], ch[2]], 0)
        elif yi == 17:
            v = jnp.concatenate([ch[1], ch[3]], 0)
        else:
            v = jnp.concatenate([xh[side, c, pl.ds(yi - 1, 1), :] for side in range(2) for c in range(16)], 0)
        hi, lo = hilo(v)
        b[384:480, yi * 128:yi * 128 + 128] = jnp.concatenate([hi, hi, lo], 0)

    lax.fori_loop(0, 8, conv, 0)

    for t in range(4):
        g3[t, 72:96, :] = jnp.zeros((24, 128), F32)
    pltpu.make_async_copy(rc, rc, c_r).wait()
    for r in range(72):
        t8, u8 = r // 9, r % 9
        g3[0, r:r + 1, :] = rc[8 * t8 + max(u8 - 1, 0), 1 if u8 == 1 else 0]
    dcopies = []
    for step in (2, 1, 3):
        yt = (y + step) % 4
        copy = remote(g3.at[0, pl.ds(0, 72)], g3.at[4 - step, pl.ds(0, 72)], d_s.at[step - 1], d_r.at[4 - step],
                      gx, yt * 4 + jj)
        copy.start()
        dcopies.append(copy)
    copies[4].wait()
    copies[6].wait()
    for copy in dcopies:
        copy.wait_recv()

    ucopies = [remote(u.at[1, pl.ds(48 * n, 48)], ur.at[pl.ds(48 * n, 48)], u_s.at[n], u_r.at[n], gx, partner)
               for n in range(4)]
    half16 = lax.broadcasted_iota(jnp.int32, (16, 128), 1) < 64
    for k in range(12):
        v = jnp.concatenate([g3[(t - y + 4) % 4, pl.ds(k, 8, stride=12), :] for t in range(4)], 0)
        v = jnp.concatenate([v, pltpu.roll(v, 64, 1)], 0)
        hi, lo = hilo(v)
        r = mm(lyi_v[...], jnp.concatenate([hi, hi, lo], 0))
        for part in range(2):
            v = jnp.where(half16, r[16 * part:16 * part + 16], r[32 + 16 * part:48 + 16 * part])
            for dst in range(2):
                u[dst, 16 * k + 8 * part:16 * k + 8 * part + 8, :] = v[8 * dst:8 * dst + 8]
        if k % 3 == 2:
            ucopies[k // 3].start()

    zero8 = jnp.zeros((8, 128), F32)

    def finish(v, hh, yy, act):
        hi, lo = hilo(jnp.concatenate([v, zero8], 0))
        r = mm(jnp.concatenate([hi, hi, lo], 0), tzi_v[...], (((0,), (0,)), ((), ())))
        for yp in range(2):
            yr = 2 * yy + yp
            t = r[64 * yp:64 * yp + 64] + co[pl.ds(pl.multiple_of(yr * 128 + hh * 64, 64), 64), :]
            t = gelu(t) if act else t
            for c in range(8):
                v_out[pl.ds(hh * 1024 + c * 128 + yr, 8, stride=16), :] = t[8 * c:8 * c + 8]

    for yy in range(8):
        finish(u[0, pl.ds(yy, 24, stride=8), :], s, yy, True)
    for copy in ucopies:
        copy.wait_recv()
    for yy in range(8):
        finish(ur[pl.ds(yy, 24, stride=8), :], 1 - s, yy, False)

    for copy in acopies + ucopies + halos + ycopies + dcopies:
        copy.wait_send()

    for mine, slot, p, copy in wcopies:
        @pl.when(jnp.logical_not(mine))
        def _():
            copy.wait_send()

    part = rb.at[pl.ds(0, 63)]
    pltpu.make_async_copy(part, part, b_s).wait()
    pltpu.make_async_copy(part, part, c_s).wait()


def gelu_kernel(v, out_hbm, outv, sem):
    s = lax.axis_index("gy") % 2
    ready = pl.ds(pl.multiple_of(s * 1024, 1024), 1024)
    copies = [pltpu.make_async_copy(v.at[ready], out_hbm.at[ready], sem.at[4])]
    copies[0].start()
    for n in range(4):
        start = pl.multiple_of((1 - s) * 1024 + 256 * n, 256)
        for m in range(4):
            outv[pl.ds(256 * n + 64 * m, 64), :] = gelu(v[pl.ds(start + 64 * m, 64), :])
        copy = pltpu.make_async_copy(outv.at[pl.ds(256 * n, 256)], out_hbm.at[pl.ds(start, 256)], sem.at[n])
        copy.start()
        copies.append(copy)
    for copy in copies:
        copy.wait()


def shards(features, conv_weight, mix_weight):
    f2 = features.reshape(2048, 128)
    f3 = features.reshape(16, 128, 128)
    w = mix_weight.reshape(512, 27)
    cw = conv_weight.transpose(1, 2, 0).reshape(256, 27)
    consts = [jnp.asarray(TABLES[n]) for n in NAMES]
    vm = pltpu.VMEM
    dma = pltpu.SemaphoreType.DMA
    scratch = [
        vm((2048, 128), F32), vm((512, 27), F32), vm((256, 27), F32),
        vm((24, 384), BF16), vm((96, 128), BF16), vm((2, 16, 24, 128), F32), vm((256, 256), BF16), vm((256, 256), BF16),
        vm((256, 128), BF16), vm((2, 256, 128), BF16), vm((3, 8, 128), F32), vm((3, 8, 128), F32), vm((32, 27), F32),
        vm((96, 96), BF16), vm((64, 192), BF16),
        vm((27, 4, 128), F32), vm((2, 24, 4, 128), F32), vm((2, 2, 24, 256), F32), vm((512, 18 * 128), BF16), vm((1152, 512), BF16),
        vm((3, 512, 128), F32),
        vm((2, 128, 128), F32), vm((2, 128, 128), F32), vm((2, 16, 16, 128), F32), vm((4, 16, 128), F32),
        vm((4, 16, 128), F32), vm((2, 192, 128), F32), vm((192, 128), F32), vm((288, 128), F32), vm((3, 72, 128), F32),
        vm((73, 1, 128), F32), vm((64, 2, 1, 128), F32), vm((32, 2, 1, 128), F32), vm((64, 2, 1, 128), F32),
        vm((4, 96, 128), F32), vm((2, 192, 128), F32), vm((192, 128), F32), vm((2048, 128), F32),
        dma((16,)), dma((4,)), dma((4,)), dma((8,)), dma((8,)), dma((3,)), dma((3,)), dma, dma, dma, dma,
        dma((3,)), dma((4,)), dma((27,)), dma((2,)), dma((4,)), dma((4,)),
    ]
    any_spec = pl.BlockSpec(memory_space=pl.ANY)
    vmem_spec = pl.BlockSpec(memory_space=pltpu.VMEM)
    hbm_spec = pl.BlockSpec(memory_space=pltpu.HBM)
    v = pl.pallas_call(
        kernel,
        out_shape=jax.ShapeDtypeStruct((2048, 128), F32),
        in_specs=[hbm_spec] * (4 + len(NAMES)),
        out_specs=vmem_spec,
        scratch_shapes=scratch,
        compiler_params=pltpu.CompilerParams(collective_id=0, has_side_effects=True,
                                             vmem_limit_bytes=40 * 1024 * 1024),
        name="layer",
    )(*[pltpu.with_memory_space_constraint(a, pltpu.HBM) for a in (f2, f3, w, cw, *consts)])
    out = pl.pallas_call(
        gelu_kernel,
        out_shape=jax.ShapeDtypeStruct((2048, 128), F32),
        in_specs=[vmem_spec],
        out_specs=any_spec,
        scratch_shapes=[vm((1024, 128), F32), dma((5,))],
        compiler_params=pltpu.CompilerParams(vmem_limit_bytes=8 * 1024 * 1024),
        name="act",
    )(v)
    return out.reshape(features.shape)


def solution(mesh):
    in_specs = (P(None, "gx", "gy", None), P(), P(None, None, None, "gy", "gx"))
    return jax.shard_map(shards, mesh=mesh, in_specs=in_specs, out_specs=P(None, "gx", "gy", None), check_vma=False)
```

```python
import functools
import math

import jax
import jax.numpy as jnp
import numpy as np
from jax import lax
from jax.experimental import pallas as pl
from jax.experimental.pallas import tpu as pltpu
from jax.sharding import PartitionSpec as P

C, NX, NY, NZ = 16, 128, 256, 128
KX, KY, KZ = 24, 24, 12
F32, BF16 = jnp.float32, jnp.bfloat16
MESH = pl.DeviceIdType.MESH


def split(a):
    hi = round_bf16(a)
    return hi, round_bf16(np.asarray(a, np.float64) - hi)


def round_bf16(a):
    import ml_dtypes

    return np.asarray(a, np.float32).astype(ml_dtypes.bfloat16).astype(np.float64)


def bf(a):
    import ml_dtypes

    return np.asarray(a, np.float32).astype(ml_dtypes.bfloat16)


def angles(positions, frequencies, length):
    return 2.0 * math.pi * ((positions[:, None] * frequencies[None, :]) % length) / length


def kept(amount, length):
    index = np.arange(amount)
    return np.where(index < amount // 2, index, length - amount + index)


def tables():
    forward = 1.0 / math.sqrt(NX * NY * NZ)
    inverse = 1.0 / math.sqrt(KX * KY * KZ)
    az = angles(np.arange(NZ), np.arange(KZ), NZ).T
    tz = np.stack([np.cos(az), -np.sin(az)], 1).reshape(2 * KZ, NZ)
    hi, lo = split(tz * forward)
    tzf = np.concatenate([hi, lo, hi], 1)
    pad = np.zeros((8, NZ))
    hi, lo = split(np.concatenate([tz * inverse, pad], 0))
    tzi = np.concatenate([hi, lo, hi], 0)

    qs = kept(KY, NY)
    lyf = np.zeros((16, 96, 96))
    lyi = np.zeros((16, 64, 192))
    for gy in range(16):
        fwd = np.zeros((2, 2, KY, 2, 2, 8))
        inv = np.zeros((2, 2, 2, 8, 2, KY))
        for own in range(2):
            start = 16 * (gy if own == 0 else gy ^ 1)
            for yp in range(2):
                a = angles(start + 2 * np.arange(8) + yp, qs, NY)
                c, s = np.cos(a), np.sin(a)
                fwd[yp, 0, :, own, 0] = c.T
                fwd[yp, 0, :, own, 1] = s.T
                fwd[yp, 1, :, own, 0] = -s.T
                fwd[yp, 1, :, own, 1] = c.T
                re = (c, -s)
                im = (s, c)
                for v in range(2):
                    w = v if yp == 0 else 1 - v
                    inv[yp, 0, own, :, v] = re[w]
                    inv[yp, 1, own, :, v] = im[w]
        hi, lo = split(fwd.reshape(96, 32))
        lyf[gy] = np.concatenate([hi, lo, hi], 1)
        inv = np.concatenate([inv.reshape(64, 2, 4, 6), np.zeros((64, 2, 4, 2))], 3)
        hi, lo = split(inv.reshape(64, 64))
        lyi[gy] = np.concatenate([hi, lo, hi], 1)

    ax = angles(np.arange(NX), kept(KX, NX), NX).reshape(16, 8, KX)
    c = np.broadcast_to(np.cos(ax).transpose(0, 2, 1)[:, :, None, :], (16, KX, 8, 8)).reshape(16, KX, 64)
    s = np.broadcast_to(np.sin(ax).transpose(0, 2, 1)[:, :, None, :], (16, KX, 8, 8)).reshape(16, KX, 64)
    tx = np.stack([np.concatenate([c, s], 2), np.concatenate([-s, c], 2)], 0)

    core, ri, ch, x = np.unravel_index(np.arange(256), (2, 2, 8, 8))
    o, i = np.unravel_index(np.arange(256), (16, 16))
    e1 = (i[None, :] == (core * 8 + ch)[:, None]).astype(np.float64)
    e2 = (o[:, None] == (core * 8 + ch)[None, :]).astype(np.float64)
    i128 = np.arange(128) // 8
    ecol = (np.arange(256)[:, None] % 16 == i128[None, :]).astype(np.float64)
    xo = np.arange(8)[:, None]
    xi = (np.arange(128) % 8)[None, :]
    mask = np.stack([(xi - xo == a - 1) for a in range(3)], 0).astype(np.float32)
    eh = np.zeros((2, 256, 128))
    mh = np.zeros((3, 8, 128), np.float32)
    for part, (hi_lo) in enumerate("hlh"):
        for side in range(2):
            lanes = part * 32 + side * 16 + np.arange(16)
            eh[0 if hi_lo == "h" else 1, np.arange(256), lanes[np.arange(256) % 16]] = 1.0
            mh[2 * side, 0 if side == 0 else 7, lanes] = 1.0
    return dict(
        tzf=bf(tzf), tzi=bf(tzi), lyf=bf(lyf), lyi=bf(lyi), tx=tx.astype(np.float32), e1=bf(e1), e2=bf(e2),
        ecol=bf(ecol), eh=bf(eh), mask=mask, mh=mh, eye=np.eye(32, 27, dtype=np.float32),
    )


TABLES = tables()
NAMES = ("tzf", "tzi", "lyf", "lyi", "tx", "e1", "e2", "ecol", "eh", "mask", "mh", "eye")


def hilo(v):
    hi = v.astype(BF16)
    return hi, (v - hi.astype(F32)).astype(BF16)


def mm(a, b, dims=(((1,), (0,)), ((), ()))):
    return lax.dot_general(a, b, dims, preferred_element_type=F32)


def erf(x):
    x = jnp.clip(x, -3.832506856900711, 3.832506856900711)
    t = x * x
    p = 0.00022905065861350646
    for coef in (0.0034082910107109506, 0.050955695062380861, 0.18520832239976145, 1.128379143519084):
        p = p * t + coef
    q = -1.1791602954361697e-7
    for coef in (0.000023547966471313185, 0.0010179625278914885, 0.014070470171167667, 0.11098505178285362,
                 0.49746925110067538, 1.0):
        q = q * t + coef
    return x * p / q


def gelu(v):
    return 0.5 * v * (1.0 + erf(v * 0.7071067811865476))


FAR_Z = (4, 3, 5, 2, 6, 1, 7, 0)
FAR_X = (2, 1, 3, 0)


def kernel(f2, f3, w_hbm, cw, tzf, tzi, lyf, lyi, tx, e1, e2, ecol, eh, mask, mh, eye, v_out, *refs):
    (fv, wv, cwv, tzf_v, tzi_v, tx_v, e1_v, e2_v, ecol_v, eh_v, mask_v, mh_v, eye_v, lyf_v, lyi_v,
     ws, wb, wg, b, lhs, xs, yh_s, yh, xh, cs, ch, za, zr, ps, pr, rs, rb, co_s, rc, g3, u, ur, co,
     ld, a_s, a_r, h_s, h_r, y_s, y_r, b_s, b_r, c_s, c_r, d_s, d_r, w_s, w_r, u_s, u_r) = refs
    gx = lax.axis_index("gx")
    gy = lax.axis_index("gy")
    y = gy // 4
    jj = gy % 4
    s = gy % 2
    x = gx % 4
    z = (gx // 4) + 4 * (jj // 2)
    me = jj * 16 + gx
    gxm, gxp = (gx + 15) % 16, (gx + 1) % 16
    gym, gyp = (gy + 15) % 16, (gy + 1) % 16

    far = pl.multiple_of((1 - s) * 1024, 1024)
    near = pl.multiple_of(s * 1024, 1024)
    loads = [(f2.at[pl.ds(far, 1024)], fv.at[pl.ds(far, 1024)]), (w_hbm, wv), (cw, cwv), (lyf.at[gy], lyf_v), (lyi.at[gy], lyi_v), (tzf, tzf_v), (tzi, tzi_v),
             (tx, tx_v), (e1, e1_v), (e2, e2_v), (ecol, ecol_v), (eh, eh_v), (mask, mask_v), (mh, mh_v), (eye, eye_v),
             (f2.at[pl.ds(near, 1024)], fv.at[pl.ds(near, 1024)])]
    copies = [pltpu.make_async_copy(src, dst, ld.at[n]) for n, (src, dst) in enumerate(loads)]
    for n in (0, 5, 15):
        copies[n].start()

    xs4 = [(x + dx) % 4 for dx in FAR_X]
    peers = []
    for dz in FAR_Z:
        zz = (z + dz) % 8
        base, hi2 = (zz % 4) * 4, (zz // 4) * 2
        for n, dx in enumerate(FAR_X):
            for dc in (1, 0):
                if dz or dx or dc:
                    peers.append((base + xs4[n], hi2 + (s + dc) % 2))

    partner = jj + 1 - 2 * s + 4 * y
    barrier = pltpu.get_barrier_semaphore()

    def greet(px, py):
        pl.semaphore_signal(barrier, inc=1, device_id=(px, py), device_id_type=MESH)

    for px in (gxm, gx, gxp):
        for py in (gym, gyp):
            greet(px, py)
    for px, pj in peers:
        greet(px, 4 * y + pj)
    for step in (2, 1, 3):
        greet(gx, (gy + 4 * step) % 16)
    for n in (3, 1, 14, 2, 10, 11, 12, 13, 7, 8, 9, 4, 6):
        copies[n].start()

    def part(h):
        r0 = pl.multiple_of(h * 64, 64)
        for yy in range(16):
            a = jnp.concatenate([fv[pl.ds(h * 1024 + c * 128 + yy, 8, stride=16), :] for c in range(8)], 0)
            hi, lo = hilo(a)
            lanes = slice((yy + 1) * 128, (yy + 2) * 128)
            b[pl.ds(r0, 64), lanes] = hi
            b[pl.ds(r0 + 128, 64), lanes] = lo
            b[pl.ds(r0 + 256, 64), lanes] = hi
            if yy in (0, 15):
                yh_s[0 if yy == 0 else 1, pl.ds(r0, 64), :] = a

    def along_z(h):
        r0 = pl.multiple_of(h * 64, 64)
        for yy in range(8):
            l0 = (2 * yy + 1) * 128
            hi = jnp.concatenate([b[pl.ds(r0, 64), l0:l0 + 128], b[pl.ds(r0, 64), l0 + 128:l0 + 256]], 0)
            lo = jnp.concatenate([b[pl.ds(r0 + 128, 64), l0:l0 + 128], b[pl.ds(r0 + 128, 64), l0 + 128:l0 + 256]], 0)
            r = mm(tzf_v[...], jnp.concatenate([hi, hi, lo], 1), (((1,), (1,)), ((), ())))
            za[h, pl.ds(yy, 24, stride=8), :] = r

    copies[0].wait()
    part(1 - s)
    copies[5].wait()
    along_z(1 - s)
    pl.semaphore_wait(barrier, 72)

    def remote(src, dst, ssem, rsem, px, py):
        return pltpu.make_async_remote_copy(src_ref=src, dst_ref=dst, send_sem=ssem, recv_sem=rsem,
                                            device_id=(px, py), device_id_type=MESH)

    acopies = [remote(za.at[1 - s, pl.ds(48 * n, 48)], zr.at[pl.ds(48 * n, 48)], a_s.at[n], a_r.at[n], gx, partner)
               for n in range(4)]
    for copy in acopies:
        copy.start()
    halos = [
        remote(f3.at[:, pl.ds(112, 16), :], xh.at[0], h_s.at[0], h_r.at[0], gxp, gy),
        remote(f3.at[:, pl.ds(0, 16), :], xh.at[1], h_s.at[1], h_r.at[1], gxm, gy),
        remote(yh_s.at[1], yh.at[0], h_s.at[2], h_r.at[2], gx, gyp),
        remote(yh_s.at[0], yh.at[1], h_s.at[3], h_r.at[3], gx, gym),
        remote(cs.at[0], ch.at[3], h_s.at[4], h_r.at[7], gxm, gym),
        remote(cs.at[1], ch.at[2], h_s.at[5], h_r.at[6], gxm, gyp),
        remote(cs.at[2], ch.at[1], h_s.at[6], h_r.at[5], gxp, gym),
        remote(cs.at[3], ch.at[0], h_s.at[7], h_r.at[4], gxp, gyp),
    ]
    for copy in halos[0:2]:
        copy.start()
    copies[15].wait()
    part(s)

    for n, (x0, y0) in enumerate(((0, 0), (0, 15), (7, 0), (7, 15))):
        cs[n] = jnp.concatenate([fv[pl.ds(c * 128 + x0 * 16 + y0, 1), :] for c in range(16)], 0)
    @pl.when(jj != 3)
    def _():
        halos[2].start()

    @pl.when(jj != 0)
    def _():
        halos[3].start()

    along_z(s)

    copies[1].wait()
    copies[14].wait()
    for n in range(4):
        t = lax.dot_general(eye_v[...], wv[pl.ds(128 * n, 128), :], (((1,), (1,)), ((), ())),
                            precision=lax.Precision.HIGHEST, preferred_element_type=F32)
        for m in range(27):
            ws[m, n, :] = t[m, :]

    odd = gx % 2 == 1

    def w_copy(m):
        picks = []
        for mode in (m, m + 27):
            l = mode % 18
            d = 8 * (l // 9) + max(l % 9 - 1, 0)
            picks.append((d, int(l % 9 == 1), mode // 18))
        dx, slot, p = (a if a == b else jnp.where(odd, b, a) for a, b in zip(*picks))
        p = 3 * (gx // 2) + p
        mine = dx == gx
        return mine, slot, p, remote(ws.at[m], wb.at[slot, p], w_s.at[m], w_r.at[slot], dx, gy)

    wcopies = [w_copy(m) for m in range(27)]
    for m, (mine, slot, p, copy) in enumerate(wcopies):
        @pl.when(jnp.logical_not(mine))
        def _():
            copy.start()

        @pl.when(mine)
        def _():
            pltpu.make_async_copy(ws.at[m], wb.at[slot, p], w_r.at[slot]).start()

    copies[3].wait()
    half = lax.broadcasted_iota(jnp.int32, (24, 128), 1) < 64
    for k in range(12):
        if k % 3 == 0:
            acopies[k // 3].wait_recv()
        v = jnp.concatenate([za[s, 16 * k:16 * k + 16, :], zr[16 * k:16 * k + 16, :]], 0)
        hi, lo = hilo(v)
        r = mm(lyf_v[...], jnp.concatenate([hi, hi, lo], 0))
        p0 = jnp.where(half, r[0:24], r[72:96])
        p1 = jnp.where(half, r[24:48], r[48:72])
        ps[pl.ds(k, 24, stride=12), :] = p0 + pltpu.roll(p1, 64, 1)

    ycopies = []
    for step in (2, 1, 3):
        yt = (y + step) % 4
        copy = remote(ps.at[pl.ds(pl.multiple_of(yt * 72, 8), 72), :], pr.at[step - 1], y_s.at[step - 1],
                      y_r.at[step - 1], gx, yt * 4 + jj)
        copy.start()
        ycopies.append(copy)

    rs[72] = jnp.zeros((1, 128), F32)


    for copy in ycopies:
        copy.wait_recv()
    total = ps[pl.ds(pl.multiple_of(y * 72, 8), 72), :] + pr[0] + pr[1] + pr[2]
    for r in range(72):
        rs[r, :, :] = total[r:r + 1, :]

    def b_copy(px, pj):
        d = pj * 16 + px
        u8 = d % 8
        r = 9 * (d // 8) + u8 + (u8 > 0).astype(jnp.int32)
        return rs.at[pl.ds(r, 2)], px, 4 * y + pj

    for px, pj in peers:
        src, dx, dy = b_copy(px, pj)
        remote(src, rb.at[me], b_s, b_r, dx, dy).start()
    src, _, _ = b_copy(gx, jj)
    pltpu.make_async_copy(src, rb.at[me], b_r).start()
    double = me % 8 == 0

    @pl.when(jj == 3)
    def _():
        halos[2].start()

    @pl.when(jj == 0)
    def _():
        halos[3].start()

    for copy in halos[4:]:
        copy.start()

    for n in (2, 10, 11, 12, 13):
        copies[n].wait()
    cwt = lax.dot_general(eye_v[...], cwv[...], (((1,), (1,)), ((), ())),
                          precision=lax.Precision.HIGHEST, preferred_element_type=F32)
    group = lax.broadcasted_iota(jnp.int32, (32, 256), 1) // 16
    picked = jnp.concatenate([jnp.where(group == o, cwt, 0.0) for o in range(16)], 0)
    whi, wlo = hilo(picked)
    xs[0] = mm(whi, ecol_v[...])
    xs[1] = mm(wlo, ecol_v[...])
    xs[2] = mm(whi, eh_v[0]) + mm(wlo, eh_v[1])

    def spread(op, carry):
        for t in range(3):
            ms = [mask_v[a] > 0 if t < 2 else mh_v[a] > 0 for a in range(3)]
            for yb in range(3):
                parts = []
                for oo in range(2):
                    for zc in range(3):
                        v = jnp.zeros((8, 128), F32)
                        for a in range(3) if t < 2 else (0, 2):
                            row = xs[t, pl.ds((2 * op + oo) * 32 + 9 * a + 3 * yb + zc, 1), :]
                            v = jnp.where(ms[a], jnp.broadcast_to(row, (8, 128)), v)
                        parts.append(v)
                v = jnp.concatenate(parts, 0).astype(BF16)
                rows = pl.ds(pl.multiple_of(384 * yb + 48 * op, 16), 48)
                if t == 0:
                    lhs[rows, 0:128] = v
                    lhs[rows, 128:256] = v
                else:
                    lhs[rows, 128 + 128 * t:256 + 128 * t] = v
        return carry

    lax.fori_loop(0, 8, spread, 0)

    def conv(pair, carry):
        acc = jnp.zeros((384, 256), F32)
        for t in range(3):
            lanes = pl.ds(pl.multiple_of((2 * pair + t) * 128, 128), 256)
            acc = acc + mm(lhs[384 * t:384 * t + 384, :], b[:, lanes])
        for n in range(2):
            v = acc[:, 128 * n:128 * n + 128].reshape(16, 3, 8, 128)
            v0, v1, v2 = (v[:, i].reshape(128, 128) for i in range(3))
            v = v1 + pltpu.roll(v0, 1, 1) + pltpu.roll(v2, 127, 1)
            co[pl.ds(pl.multiple_of((2 * pair + n) * 128, 128), 128), :] = v
        return carry

    for n in (7, 8, 9):
        copies[n].wait()
    def gather(slot):
        pltpu.make_async_copy(wb.at[slot], wb.at[slot], w_r.at[slot]).wait()
        for t in range(4):
            for p in range(24):
                wg[slot, t // 2, p:p + 1, 128 * (t % 2):128 * (t % 2) + 128] = wb[slot, p, t:t + 1, :]

    gather(0)

    @pl.when(double)
    def _():
        gather(1)

    pltpu.make_async_copy(rb, rb, b_r).wait()

    def mix(slots):
        accs = [[[jnp.zeros((24, 128), F32) for _ in range(2)] for _ in range(2)] for _ in slots]
        for g in range(16):
            for core in range(2):
                for n, slot in enumerate(slots):
                    row = rb[16 * core + g, slot] + rb[16 * core + 32 + g, slot]
                    row = jnp.broadcast_to(row, (24, 128))
                    for part in range(2):
                        accs[n][part][core] = accs[n][part][core] + tx_v[part, g] * row
        acc = jnp.concatenate([jnp.concatenate(accs[n][part], 1) for n in range(len(slots)) for part in range(2)], 0)
        size = 48 * len(slots)
        hi, lo = hilo(acc)
        cc = mm(jnp.concatenate([hi, lo], 0), e1_v[...])
        cc = cc[0:size] + cc[size:2 * size]
        prods = []
        for n, slot in enumerate(slots):
            cr, ci = cc[48 * n:48 * n + 24], cc[48 * n + 24:48 * n + 48]
            wr, wi = wg[slot, 0], wg[slot, 1]
            prods += [wr * cr - wi * ci, wr * ci + wi * cr]
        hi, lo = hilo(jnp.concatenate(prods, 0))
        mx = mm(jnp.concatenate([hi, lo], 0), e2_v[...])
        mx = mx[0:size] + mx[size:2 * size]
        for dz in (4, 3, 1, 2):
            for nx, dx in enumerate(FAR_X):
                g = ((z + dz) % 4) * 4 + xs4[nx]
                for core in range(2):
                    for n, slot in enumerate(slots):
                        lanes = slice(128 * core, 128 * core + 128)
                        row = tx_v[0, g] * mx[48 * n:48 * n + 24, lanes] + tx_v[1, g] * mx[48 * n + 24:48 * n + 48, lanes]
                        co_s[2 * g + core, slot] = jnp.sum(row, axis=0, keepdims=True)
                    if len(slots) == 1:
                        co_s[2 * g + core, 1] = jnp.zeros((1, 128), F32)
                for zd in ((dz, (dz + 4) % 8) if dz != 3 else (3, 7)):
                    zz = (z + zd) % 8
                    for dc in (1, 0):
                        if zd or dx or dc:
                            pj = (zz // 4) * 2 + (s + dc) % 2
                            remote(co_s.at[2 * g + pj % 2], rc.at[me], c_s, c_r, g, 4 * y + pj).start()
        pltpu.make_async_copy(co_s.at[2 * gx + s], rc.at[me], c_r).start()

    @pl.when(double)
    def _():
        mix((0, 1))

    @pl.when(jnp.logical_not(double))
    def _():
        mix((0,))


    b[384:512, :] = jnp.zeros((128, 18 * 128), BF16)
    for copy in halos:
        copy.wait_recv()
    for yi, side in ((0, 0), (17, 1)):
        hi, lo = hilo(yh[side])
        lanes = slice(yi * 128, yi * 128 + 128)
        b[0:128, lanes] = hi
        b[128:256, lanes] = lo
        b[256:384, lanes] = hi
    for yi in range(18):
        if yi == 0:
            v = jnp.concatenate([ch[0], ch[2]], 0)
        elif yi == 17:
            v = jnp.concatenate([ch[1], ch[3]], 0)
        else:
            v = jnp.concatenate([xh[side, c, pl.ds(yi - 1, 1), :] for side in range(2) for c in range(16)], 0)
        hi, lo = hilo(v)
        b[384:480, yi * 128:yi * 128 + 128] = jnp.concatenate([hi, hi, lo], 0)

    lax.fori_loop(0, 8, conv, 0)

    for t in range(4):
        g3[t, 72:96, :] = jnp.zeros((24, 128), F32)
    pltpu.make_async_copy(rc, rc, c_r).wait()
    for r in range(72):
        t8, u8 = r // 9, r % 9
        g3[0, r:r + 1, :] = rc[8 * t8 + max(u8 - 1, 0), 1 if u8 == 1 else 0]
    dcopies = []
    for step in (2, 1, 3):
        yt = (y + step) % 4
        copy = remote(g3.at[0, pl.ds(0, 72)], g3.at[4 - step, pl.ds(0, 72)], d_s.at[step - 1], d_r.at[4 - step],
                      gx, yt * 4 + jj)
        copy.start()
        dcopies.append(copy)
    copies[4].wait()
    copies[6].wait()
    for copy in dcopies:
        copy.wait_recv()

    ucopies = [remote(u.at[1, pl.ds(48 * n, 48)], ur.at[pl.ds(48 * n, 48)], u_s.at[n], u_r.at[n], gx, partner)
               for n in range(4)]
    half16 = lax.broadcasted_iota(jnp.int32, (16, 128), 1) < 64
    for k in range(12):
        v = jnp.concatenate([g3[(t - y + 4) % 4, pl.ds(k, 8, stride=12), :] for t in range(4)], 0)
        v = jnp.concatenate([v, pltpu.roll(v, 64, 1)], 0)
        hi, lo = hilo(v)
        r = mm(lyi_v[...], jnp.concatenate([hi, hi, lo], 0))
        for part in range(2):
            v = jnp.where(half16, r[16 * part:16 * part + 16], r[32 + 16 * part:48 + 16 * part])
            for dst in range(2):
                u[dst, 16 * k + 8 * part:16 * k + 8 * part + 8, :] = v[8 * dst:8 * dst + 8]
        if k % 3 == 2:
            ucopies[k // 3].start()

    zero8 = jnp.zeros((8, 128), F32)

    def finish(v, hh, yy, act):
        hi, lo = hilo(jnp.concatenate([v, zero8], 0))
        r = mm(jnp.concatenate([hi, hi, lo], 0), tzi_v[...], (((0,), (0,)), ((), ())))
        for yp in range(2):
            yr = 2 * yy + yp
            t = r[64 * yp:64 * yp + 64] + co[pl.ds(pl.multiple_of(yr * 128 + hh * 64, 64), 64), :]
            t = gelu(t) if act else t
            for c in range(8):
                v_out[pl.ds(hh * 1024 + c * 128 + yr, 8, stride=16), :] = t[8 * c:8 * c + 8]

    for yy in range(8):
        finish(u[0, pl.ds(yy, 24, stride=8), :], s, yy, True)
    for copy in ucopies:
        copy.wait_recv()
    for yy in range(8):
        finish(ur[pl.ds(yy, 24, stride=8), :], 1 - s, yy, True)

    for copy in acopies + ucopies + halos + ycopies + dcopies:
        copy.wait_send()

    for mine, slot, p, copy in wcopies:
        @pl.when(jnp.logical_not(mine))
        def _():
            copy.wait_send()

    part = rb.at[pl.ds(0, 63)]
    pltpu.make_async_copy(part, part, b_s).wait()
    pltpu.make_async_copy(part, part, c_s).wait()


def copy_kernel(v, out_hbm, sem):
    copies = [pltpu.make_async_copy(v.at[pl.ds(512 * n, 512)], out_hbm.at[pl.ds(512 * n, 512)], sem.at[n])
              for n in range(4)]
    for copy in copies:
        copy.start()
    for copy in copies:
        copy.wait()


def shards(features, conv_weight, mix_weight):
    f2 = features.reshape(2048, 128)
    f3 = features.reshape(16, 128, 128)
    w = mix_weight.reshape(512, 27)
    cw = conv_weight.transpose(1, 2, 0).reshape(256, 27)
    consts = [jnp.asarray(TABLES[n]) for n in NAMES]
    vm = pltpu.VMEM
    dma = pltpu.SemaphoreType.DMA
    scratch = [
        vm((2048, 128), F32), vm((512, 27), F32), vm((256, 27), F32),
        vm((24, 384), BF16), vm((96, 128), BF16), vm((2, 16, 24, 128), F32), vm((256, 256), BF16), vm((256, 256), BF16),
        vm((256, 128), BF16), vm((2, 256, 128), BF16), vm((3, 8, 128), F32), vm((3, 8, 128), F32), vm((32, 27), F32),
        vm((96, 96), BF16), vm((64, 192), BF16),
        vm((27, 4, 128), F32), vm((2, 24, 4, 128), F32), vm((2, 2, 24, 256), F32), vm((512, 18 * 128), BF16), vm((1152, 512), BF16),
        vm((3, 512, 128), F32),
        vm((2, 128, 128), F32), vm((2, 128, 128), F32), vm((2, 16, 16, 128), F32), vm((4, 16, 128), F32),
        vm((4, 16, 128), F32), vm((2, 192, 128), F32), vm((192, 128), F32), vm((288, 128), F32), vm((3, 72, 128), F32),
        vm((73, 1, 128), F32), vm((64, 2, 1, 128), F32), vm((32, 2, 1, 128), F32), vm((64, 2, 1, 128), F32),
        vm((4, 96, 128), F32), vm((2, 192, 128), F32), vm((192, 128), F32), vm((2048, 128), F32),
        dma((16,)), dma((4,)), dma((4,)), dma((8,)), dma((8,)), dma((3,)), dma((3,)), dma, dma, dma, dma,
        dma((3,)), dma((4,)), dma((27,)), dma((2,)), dma((4,)), dma((4,)),
    ]
    any_spec = pl.BlockSpec(memory_space=pl.ANY)
    vmem_spec = pl.BlockSpec(memory_space=pltpu.VMEM)
    hbm_spec = pl.BlockSpec(memory_space=pltpu.HBM)
    v = pl.pallas_call(
        kernel,
        out_shape=jax.ShapeDtypeStruct((2048, 128), F32),
        in_specs=[hbm_spec] * (4 + len(NAMES)),
        out_specs=vmem_spec,
        scratch_shapes=scratch,
        compiler_params=pltpu.CompilerParams(collective_id=0, has_side_effects=True,
                                             vmem_limit_bytes=40 * 1024 * 1024),
        name="layer",
    )(*[pltpu.with_memory_space_constraint(a, pltpu.HBM) for a in (f2, f3, w, cw, *consts)])
    out = pl.pallas_call(
        copy_kernel,
        out_shape=jax.ShapeDtypeStruct((2048, 128), F32),
        in_specs=[vmem_spec],
        out_specs=any_spec,
        scratch_shapes=[dma((4,))],
        compiler_params=pltpu.CompilerParams(vmem_limit_bytes=8 * 1024 * 1024),
        name="act",
    )(v)
    return out.reshape(features.shape)


def solution(mesh):
    in_specs = (P(None, "gx", "gy", None), P(), P(None, None, None, "gy", "gx"))
    return jax.shard_map(shards, mesh=mesh, in_specs=in_specs, out_specs=P(None, "gx", "gy", None), check_vma=False)
```

```python
import functools
import math

import jax
import jax.numpy as jnp
import numpy as np
from jax import lax
from jax.experimental import pallas as pl
from jax.experimental.pallas import tpu as pltpu
from jax.sharding import PartitionSpec as P

C, NX, NY, NZ = 16, 128, 256, 128
KX, KY, KZ = 24, 24, 12
F32, BF16 = jnp.float32, jnp.bfloat16
MESH = pl.DeviceIdType.MESH


def split(a):
    hi = round_bf16(a)
    return hi, round_bf16(np.asarray(a, np.float64) - hi)


def round_bf16(a):
    import ml_dtypes

    return np.asarray(a, np.float32).astype(ml_dtypes.bfloat16).astype(np.float64)


def bf(a):
    import ml_dtypes

    return np.asarray(a, np.float32).astype(ml_dtypes.bfloat16)


def angles(positions, frequencies, length):
    return 2.0 * math.pi * ((positions[:, None] * frequencies[None, :]) % length) / length


def kept(amount, length):
    index = np.arange(amount)
    return np.where(index < amount // 2, index, length - amount + index)


def tables():
    forward = 1.0 / math.sqrt(NX * NY * NZ)
    inverse = 1.0 / math.sqrt(KX * KY * KZ)
    az = angles(np.arange(NZ), np.arange(KZ), NZ).T
    tz = np.stack([np.cos(az), -np.sin(az)], 1).reshape(2 * KZ, NZ)
    hi, lo = split(tz * forward)
    tzf = np.concatenate([hi, lo, hi], 1)
    pad = np.zeros((8, NZ))
    hi, lo = split(np.concatenate([tz * inverse, pad], 0))
    tzi = np.concatenate([hi, lo, hi], 0)

    qs = kept(KY, NY)
    lyf = np.zeros((16, 96, 96))
    lyi = np.zeros((16, 64, 192))
    for gy in range(16):
        fwd = np.zeros((2, 2, KY, 2, 2, 8))
        inv = np.zeros((2, 2, 2, 8, 2, KY))
        for own in range(2):
            start = 16 * (gy if own == 0 else gy ^ 1)
            for yp in range(2):
                a = angles(start + 2 * np.arange(8) + yp, qs, NY)
                c, s = np.cos(a), np.sin(a)
                fwd[yp, 0, :, own, 0] = c.T
                fwd[yp, 0, :, own, 1] = s.T
                fwd[yp, 1, :, own, 0] = -s.T
                fwd[yp, 1, :, own, 1] = c.T
                re = (c, -s)
                im = (s, c)
                for v in range(2):
                    w = v if yp == 0 else 1 - v
                    inv[yp, 0, own, :, v] = re[w]
                    inv[yp, 1, own, :, v] = im[w]
        hi, lo = split(fwd.reshape(96, 32))
        lyf[gy] = np.concatenate([hi, lo, hi], 1)
        inv = np.concatenate([inv.reshape(64, 2, 4, 6), np.zeros((64, 2, 4, 2))], 3)
        hi, lo = split(inv.reshape(64, 64))
        lyi[gy] = np.concatenate([hi, lo, hi], 1)

    ax = angles(np.arange(NX), kept(KX, NX), NX).reshape(16, 8, KX)
    c = np.broadcast_to(np.cos(ax).transpose(0, 2, 1)[:, :, None, :], (16, KX, 8, 8)).reshape(16, KX, 64)
    s = np.broadcast_to(np.sin(ax).transpose(0, 2, 1)[:, :, None, :], (16, KX, 8, 8)).reshape(16, KX, 64)
    tx = np.stack([np.concatenate([c, s], 2), np.concatenate([-s, c], 2)], 0)

    core, ri, ch, x = np.unravel_index(np.arange(256), (2, 2, 8, 8))
    o, i = np.unravel_index(np.arange(256), (16, 16))
    e1 = (i[None, :] == (core * 8 + ch)[:, None]).astype(np.float64)
    e2 = (o[:, None] == (core * 8 + ch)[None, :]).astype(np.float64)
    i128 = np.arange(128) // 8
    ecol = (np.arange(256)[:, None] % 16 == i128[None, :]).astype(np.float64)
    xo = np.arange(8)[:, None]
    xi = (np.arange(128) % 8)[None, :]
    mask = np.stack([(xi - xo == a - 1) for a in range(3)], 0).astype(np.float32)
    eh = np.zeros((2, 256, 128))
    mh = np.zeros((3, 8, 128), np.float32)
    for part, (hi_lo) in enumerate("hlh"):
        for side in range(2):
            lanes = part * 32 + side * 16 + np.arange(16)
            eh[0 if hi_lo == "h" else 1, np.arange(256), lanes[np.arange(256) % 16]] = 1.0
            mh[2 * side, 0 if side == 0 else 7, lanes] = 1.0
    return dict(
        tzf=bf(tzf), tzi=bf(tzi), lyf=bf(lyf), lyi=bf(lyi), tx=tx.astype(np.float32), e1=bf(e1), e2=bf(e2),
        ecol=bf(ecol), eh=bf(eh), mask=mask, mh=mh, eye=np.eye(32, 27, dtype=np.float32),
    )


TABLES = tables()
NAMES = ("tzf", "tzi", "lyf", "lyi", "tx", "e1", "e2", "ecol", "eh", "mask", "mh", "eye")


def hilo(v):
    hi = v.astype(BF16)
    return hi, (v - hi.astype(F32)).astype(BF16)


def mm(a, b, dims=(((1,), (0,)), ((), ()))):
    return lax.dot_general(a, b, dims, preferred_element_type=F32)


def erf(x):
    x = jnp.clip(x, -3.832506856900711, 3.832506856900711)
    t = x * x
    p = 0.00022905065861350646
    for coef in (0.0034082910107109506, 0.050955695062380861, 0.18520832239976145, 1.128379143519084):
        p = p * t + coef
    q = -1.1791602954361697e-7
    for coef in (0.000023547966471313185, 0.0010179625278914885, 0.014070470171167667, 0.11098505178285362,
                 0.49746925110067538, 1.0):
        q = q * t + coef
    return x * p / q


def gelu(v):
    return 0.5 * v * (1.0 + erf(v * 0.7071067811865476))


FAR_Z = (4, 3, 5, 2, 6, 1, 7, 0)
FAR_X = (2, 1, 3, 0)


def kernel(f2, f3, w_hbm, cw, tzf, tzi, lyf, lyi, tx, e1, e2, ecol, eh, mask, mh, eye, v_out, *refs):
    (fv, wv, cwv, tzf_v, tzi_v, tx_v, e1_v, e2_v, ecol_v, eh_v, mask_v, mh_v, eye_v, lyf_v, lyi_v,
     ws, wb, wg, b, lhs, xs, yh_s, yh, xh, cs, ch, za, zr, ps, pr, rs, rb, co_s, rc, g3, u, ur, co,
     ld, a_s, a_r, h_s, h_r, y_s, y_r, b_s, b_r, c_s, c_r, d_s, d_r, w_s, w_r, u_s, u_r) = refs
    gx = lax.axis_index("gx")
    gy = lax.axis_index("gy")
    y = gy // 4
    jj = gy % 4
    s = gy % 2
    x = gx % 4
    z = (gx // 4) + 4 * (jj // 2)
    me = jj * 16 + gx
    gxm, gxp = (gx + 15) % 16, (gx + 1) % 16
    gym, gyp = (gy + 15) % 16, (gy + 1) % 16

    far = pl.multiple_of((1 - s) * 1024, 1024)
    near = pl.multiple_of(s * 1024, 1024)
    loads = [(f2.at[pl.ds(far, 1024)], fv.at[pl.ds(far, 1024)]), (w_hbm, wv), (cw, cwv), (lyf.at[gy], lyf_v), (lyi.at[gy], lyi_v), (tzf, tzf_v), (tzi, tzi_v),
             (tx, tx_v), (e1, e1_v), (e2, e2_v), (ecol, ecol_v), (eh, eh_v), (mask, mask_v), (mh, mh_v), (eye, eye_v),
             (f2.at[pl.ds(near, 1024)], fv.at[pl.ds(near, 1024)])]
    copies = [pltpu.make_async_copy(src, dst, ld.at[n]) for n, (src, dst) in enumerate(loads)]
    for n in (0, 5, 15):
        copies[n].start()

    xs4 = [(x + dx) % 4 for dx in FAR_X]
    peers = []
    for dz in FAR_Z:
        zz = (z + dz) % 8
        base, hi2 = (zz % 4) * 4, (zz // 4) * 2
        for n, dx in enumerate(FAR_X):
            for dc in (1, 0):
                if dz or dx or dc:
                    peers.append((base + xs4[n], hi2 + (s + dc) % 2))

    partner = jj + 1 - 2 * s + 4 * y
    barrier = pltpu.get_barrier_semaphore()

    def greet(px, py):
        pl.semaphore_signal(barrier, inc=1, device_id=(px, py), device_id_type=MESH)

    for px in (gxm, gx, gxp):
        for py in (gym, gyp):
            greet(px, py)
    for px, pj in peers:
        greet(px, 4 * y + pj)
    for step in (2, 1, 3):
        greet(gx, (gy + 4 * step) % 16)
    for n in (3, 1, 14, 2, 10, 11, 12, 13, 7, 8, 9, 4, 6):
        copies[n].start()

    def part(h):
        r0 = pl.multiple_of(h * 64, 64)
        for yy in range(16):
            a = jnp.concatenate([fv[pl.ds(h * 1024 + c * 128 + yy, 8, stride=16), :] for c in range(8)], 0)
            hi, lo = hilo(a)
            lanes = slice((yy + 1) * 128, (yy + 2) * 128)
            b[pl.ds(r0, 64), lanes] = hi
            b[pl.ds(r0 + 128, 64), lanes] = lo
            b[pl.ds(r0 + 256, 64), lanes] = hi
            if yy in (0, 15):
                yh_s[0 if yy == 0 else 1, pl.ds(r0, 64), :] = a

    def along_z(h):
        r0 = pl.multiple_of(h * 64, 64)
        for yy in range(8):
            l0 = (2 * yy + 1) * 128
            hi = jnp.concatenate([b[pl.ds(r0, 64), l0:l0 + 128], b[pl.ds(r0, 64), l0 + 128:l0 + 256]], 0)
            lo = jnp.concatenate([b[pl.ds(r0 + 128, 64), l0:l0 + 128], b[pl.ds(r0 + 128, 64), l0 + 128:l0 + 256]], 0)
            r = mm(tzf_v[...], jnp.concatenate([hi, hi, lo], 1), (((1,), (1,)), ((), ())))
            za[h, pl.ds(yy, 24, stride=8), :] = r

    copies[0].wait()
    part(1 - s)
    copies[5].wait()
    along_z(1 - s)
    pl.semaphore_wait(barrier, 72)

    def remote(src, dst, ssem, rsem, px, py):
        return pltpu.make_async_remote_copy(src_ref=src, dst_ref=dst, send_sem=ssem, recv_sem=rsem,
                                            device_id=(px, py), device_id_type=MESH)

    acopies = [remote(za.at[1 - s, pl.ds(48 * n, 48)], zr.at[pl.ds(48 * n, 48)], a_s.at[n], a_r.at[n], gx, partner)
               for n in range(4)]
    for copy in acopies:
        copy.start()
    halos = [
        remote(f3.at[:, pl.ds(112, 16), :], xh.at[0], h_s.at[0], h_r.at[0], gxp, gy),
        remote(f3.at[:, pl.ds(0, 16), :], xh.at[1], h_s.at[1], h_r.at[1], gxm, gy),
        remote(yh_s.at[1], yh.at[0], h_s.at[2], h_r.at[2], gx, gyp),
        remote(yh_s.at[0], yh.at[1], h_s.at[3], h_r.at[3], gx, gym),
        remote(cs.at[0], ch.at[3], h_s.at[4], h_r.at[7], gxm, gym),
        remote(cs.at[1], ch.at[2], h_s.at[5], h_r.at[6], gxm, gyp),
        remote(cs.at[2], ch.at[1], h_s.at[6], h_r.at[5], gxp, gym),
        remote(cs.at[3], ch.at[0], h_s.at[7], h_r.at[4], gxp, gyp),
    ]
    for copy in halos[0:2]:
        copy.start()
    copies[15].wait()
    part(s)

    for n, (x0, y0) in enumerate(((0, 0), (0, 15), (7, 0), (7, 15))):
        cs[n] = jnp.concatenate([fv[pl.ds(c * 128 + x0 * 16 + y0, 1), :] for c in range(16)], 0)
    @pl.when(jj != 3)
    def _():
        halos[2].start()

    @pl.when(jj != 0)
    def _():
        halos[3].start()

    along_z(s)

    copies[1].wait()
    copies[14].wait()
    for n in range(4):
        t = lax.dot_general(eye_v[...], wv[pl.ds(128 * n, 128), :], (((1,), (1,)), ((), ())),
                            precision=lax.Precision.HIGHEST, preferred_element_type=F32)
        for m in range(27):
            ws[m, n, :] = t[m, :]

    odd = gx % 2 == 1

    def w_copy(m):
        picks = []
        for mode in (m, m + 27):
            l = mode % 18
            d = 8 * (l // 9) + max(l % 9 - 1, 0)
            picks.append((d, int(l % 9 == 1), mode // 18))
        dx, slot, p = (a if a == b else jnp.where(odd, b, a) for a, b in zip(*picks))
        p = 3 * (gx // 2) + p
        mine = dx == gx
        return mine, slot, p, remote(ws.at[m], wb.at[slot, p], w_s.at[m], w_r.at[slot], dx, gy)

    wcopies = [w_copy(m) for m in range(27)]
    for m, (mine, slot, p, copy) in enumerate(wcopies):
        @pl.when(jnp.logical_not(mine))
        def _():
            copy.start()

        @pl.when(mine)
        def _():
            pltpu.make_async_copy(ws.at[m], wb.at[slot, p], w_r.at[slot]).start()

    copies[3].wait()
    half = lax.broadcasted_iota(jnp.int32, (24, 128), 1) < 64
    for k in range(12):
        if k % 3 == 0:
            acopies[k // 3].wait_recv()
        v = jnp.concatenate([za[s, 16 * k:16 * k + 16, :], zr[16 * k:16 * k + 16, :]], 0)
        hi, lo = hilo(v)
        r = mm(lyf_v[...], jnp.concatenate([hi, hi, lo], 0))
        p0 = jnp.where(half, r[0:24], r[72:96])
        p1 = jnp.where(half, r[24:48], r[48:72])
        ps[pl.ds(k, 24, stride=12), :] = p0 + pltpu.roll(p1, 64, 1)

    ycopies = []
    for step in (2, 1, 3):
        yt = (y + step) % 4
        copy = remote(ps.at[pl.ds(pl.multiple_of(yt * 72, 8), 72), :], pr.at[step - 1], y_s.at[step - 1],
                      y_r.at[step - 1], gx, yt * 4 + jj)
        copy.start()
        ycopies.append(copy)

    rs[72] = jnp.zeros((1, 128), F32)


    for copy in ycopies:
        copy.wait_recv()
    total = ps[pl.ds(pl.multiple_of(y * 72, 8), 72), :] + pr[0] + pr[1] + pr[2]
    for r in range(72):
        rs[r, :, :] = total[r:r + 1, :]

    def b_copy(px, pj):
        d = pj * 16 + px
        u8 = d % 8
        r = 9 * (d // 8) + u8 + (u8 > 0).astype(jnp.int32)
        return rs.at[pl.ds(r, 2)], px, 4 * y + pj

    for px, pj in peers:
        src, dx, dy = b_copy(px, pj)
        remote(src, rb.at[me], b_s, b_r, dx, dy).start()
    src, _, _ = b_copy(gx, jj)
    pltpu.make_async_copy(src, rb.at[me], b_r).start()
    double = me % 8 == 0

    @pl.when(jj == 3)
    def _():
        halos[2].start()

    @pl.when(jj == 0)
    def _():
        halos[3].start()

    for copy in halos[4:]:
        copy.start()

    for n in (2, 10, 11, 12, 13):
        copies[n].wait()
    cwt = lax.dot_general(eye_v[...], cwv[...], (((1,), (1,)), ((), ())),
                          precision=lax.Precision.HIGHEST, preferred_element_type=F32)
    group = lax.broadcasted_iota(jnp.int32, (32, 256), 1) // 16
    picked = jnp.concatenate([jnp.where(group == o, cwt, 0.0) for o in range(16)], 0)
    whi, wlo = hilo(picked)
    xs[0] = mm(whi, ecol_v[...])
    xs[1] = mm(wlo, ecol_v[...])
    xs[2] = mm(whi, eh_v[0]) + mm(wlo, eh_v[1])

    def spread(op, carry):
        for t in range(3):
            ms = [mask_v[a] > 0 if t < 2 else mh_v[a] > 0 for a in range(3)]
            for yb in range(3):
                parts = []
                for oo in range(2):
                    for zc in range(3):
                        v = jnp.zeros((8, 128), F32)
                        for a in range(3) if t < 2 else (0, 2):
                            row = xs[t, pl.ds((2 * op + oo) * 32 + 9 * a + 3 * yb + zc, 1), :]
                            v = jnp.where(ms[a], jnp.broadcast_to(row, (8, 128)), v)
                        parts.append(v)
                v = jnp.concatenate(parts, 0).astype(BF16)
                rows = pl.ds(pl.multiple_of(384 * yb + 48 * op, 16), 48)
                if t == 0:
                    lhs[rows, 0:128] = v
                    lhs[rows, 128:256] = v
                else:
                    lhs[rows, 128 + 128 * t:256 + 128 * t] = v
        return carry

    lax.fori_loop(0, 8, spread, 0)

    def conv(pair, carry):
        acc = jnp.zeros((384, 256), F32)
        for t in range(3):
            lanes = pl.ds(pl.multiple_of((2 * pair + t) * 128, 128), 256)
            acc = acc + mm(lhs[384 * t:384 * t + 384, :], b[:, lanes])
        for n in range(2):
            v = acc[:, 128 * n:128 * n + 128].reshape(16, 3, 8, 128)
            v0, v1, v2 = (v[:, i].reshape(128, 128) for i in range(3))
            v = v1 + pltpu.roll(v0, 1, 1) + pltpu.roll(v2, 127, 1)
            co[pl.ds(pl.multiple_of((2 * pair + n) * 128, 128), 128), :] = v
        return carry

    for n in (7, 8, 9):
        copies[n].wait()
    def gather(slot):
        pltpu.make_async_copy(wb.at[slot], wb.at[slot], w_r.at[slot]).wait()
        for t in range(4):
            for p in range(24):
                wg[slot, t // 2, p:p + 1, 128 * (t % 2):128 * (t % 2) + 128] = wb[slot, p, t:t + 1, :]

    gather(0)

    @pl.when(double)
    def _():
        gather(1)

    pltpu.make_async_copy(rb, rb, b_r).wait()

    def mix(slots):
        accs = [[[jnp.zeros((24, 128), F32) for _ in range(2)] for _ in range(2)] for _ in slots]
        for g in range(16):
            for core in range(2):
                for n, slot in enumerate(slots):
                    row = rb[16 * core + g, slot] + rb[16 * core + 32 + g, slot]
                    row = jnp.broadcast_to(row, (24, 128))
                    for part in range(2):
                        accs[n][part][core] = accs[n][part][core] + tx_v[part, g] * row
        acc = jnp.concatenate([jnp.concatenate(accs[n][part], 1) for n in range(len(slots)) for part in range(2)], 0)
        size = 48 * len(slots)
        hi, lo = hilo(acc)
        cc = mm(jnp.concatenate([hi, lo], 0), e1_v[...])
        cc = cc[0:size] + cc[size:2 * size]
        prods = []
        for n, slot in enumerate(slots):
            cr, ci = cc[48 * n:48 * n + 24], cc[48 * n + 24:48 * n + 48]
            wr, wi = wg[slot, 0], wg[slot, 1]
            prods += [wr * cr - wi * ci, wr * ci + wi * cr]
        hi, lo = hilo(jnp.concatenate(prods, 0))
        mx = mm(jnp.concatenate([hi, lo], 0), e2_v[...])
        mx = mx[0:size] + mx[size:2 * size]
        for dz in (4, 3, 1, 2):
            for nx, dx in enumerate(FAR_X):
                g = ((z + dz) % 4) * 4 + xs4[nx]
                for core in range(2):
                    for n, slot in enumerate(slots):
                        lanes = slice(128 * core, 128 * core + 128)
                        row = tx_v[0, g] * mx[48 * n:48 * n + 24, lanes] + tx_v[1, g] * mx[48 * n + 24:48 * n + 48, lanes]
                        co_s[2 * g + core, slot] = jnp.sum(row, axis=0, keepdims=True)
                    if len(slots) == 1:
                        co_s[2 * g + core, 1] = jnp.zeros((1, 128), F32)
                for zd in ((dz, (dz + 4) % 8) if dz != 3 else (3, 7)):
                    zz = (z + zd) % 8
                    for dc in (1, 0):
                        if zd or dx or dc:
                            pj = (zz // 4) * 2 + (s + dc) % 2
                            remote(co_s.at[2 * g + pj % 2], rc.at[me], c_s, c_r, g, 4 * y + pj).start()
        pltpu.make_async_copy(co_s.at[2 * gx + s], rc.at[me], c_r).start()

    @pl.when(double)
    def _():
        mix((0, 1))

    @pl.when(jnp.logical_not(double))
    def _():
        mix((0,))


    b[384:512, :] = jnp.zeros((128, 18 * 128), BF16)
    for copy in halos:
        copy.wait_recv()
    for yi, side in ((0, 0), (17, 1)):
        hi, lo = hilo(yh[side])
        lanes = slice(yi * 128, yi * 128 + 128)
        b[0:128, lanes] = hi
        b[128:256, lanes] = lo
        b[256:384, lanes] = hi
    for yi in range(18):
        if yi == 0:
            v = jnp.concatenate([ch[0], ch[2]], 0)
        elif yi == 17:
            v = jnp.concatenate([ch[1], ch[3]], 0)
        else:
            v = jnp.concatenate([xh[side, c, pl.ds(yi - 1, 1), :] for side in range(2) for c in range(16)], 0)
        hi, lo = hilo(v)
        b[384:480, yi * 128:yi * 128 + 128] = jnp.concatenate([hi, hi, lo], 0)

    lax.fori_loop(0, 8, conv, 0)

    for t in range(4):
        g3[t, 72:96, :] = jnp.zeros((24, 128), F32)
    pltpu.make_async_copy(rc, rc, c_r).wait()
    for r in range(72):
        t8, u8 = r // 9, r % 9
        g3[0, r:r + 1, :] = rc[8 * t8 + max(u8 - 1, 0), 1 if u8 == 1 else 0]
    dcopies = []
    for step in (2, 1, 3):
        yt = (y + step) % 4
        copy = remote(g3.at[0, pl.ds(0, 72)], g3.at[4 - step, pl.ds(0, 72)], d_s.at[step - 1], d_r.at[4 - step],
                      gx, yt * 4 + jj)
        copy.start()
        dcopies.append(copy)
    copies[4].wait()
    copies[6].wait()
    for copy in dcopies:
        copy.wait_recv()

    ucopies = [remote(u.at[1, pl.ds(48 * n, 48)], ur.at[pl.ds(48 * n, 48)], u_s.at[n], u_r.at[n], gx, partner)
               for n in range(4)]
    half16 = lax.broadcasted_iota(jnp.int32, (16, 128), 1) < 64
    for k in range(12):
        v = jnp.concatenate([g3[(t - y + 4) % 4, pl.ds(k, 8, stride=12), :] for t in range(4)], 0)
        v = jnp.concatenate([v, pltpu.roll(v, 64, 1)], 0)
        hi, lo = hilo(v)
        r = mm(lyi_v[...], jnp.concatenate([hi, hi, lo], 0))
        for part in range(2):
            v = jnp.where(half16, r[16 * part:16 * part + 16], r[32 + 16 * part:48 + 16 * part])
            for dst in range(2):
                u[dst, 16 * k + 8 * part:16 * k + 8 * part + 8, :] = v[8 * dst:8 * dst + 8]
        if k % 3 == 2:
            ucopies[k // 3].start()

    zero8 = jnp.zeros((8, 128), F32)

    def finish(v, hh, yy, act):
        hi, lo = hilo(jnp.concatenate([v, zero8], 0))
        r = mm(jnp.concatenate([hi, hi, lo], 0), tzi_v[...], (((0,), (0,)), ((), ())))
        for yp in range(2):
            yr = 2 * yy + yp
            t = r[64 * yp:64 * yp + 64] + co[pl.ds(pl.multiple_of(yr * 128 + hh * 64, 64), 64), :]
            t = gelu(t) if act else t
            for c in range(8):
                v_out[pl.ds(hh * 1024 + c * 128 + yr, 8, stride=16), :] = t[8 * c:8 * c + 8]

    for yy in range(8):
        finish(u[0, pl.ds(yy, 24, stride=8), :], s, yy, True)
    for copy in ucopies:
        copy.wait_recv()
    for yy in range(8):
        finish(ur[pl.ds(yy, 24, stride=8), :], 1 - s, yy, False)

    for copy in acopies + ucopies + halos + ycopies + dcopies:
        copy.wait_send()

    for mine, slot, p, copy in wcopies:
        @pl.when(jnp.logical_not(mine))
        def _():
            copy.wait_send()

    part = rb.at[pl.ds(0, 63)]
    pltpu.make_async_copy(part, part, b_s).wait()
    pltpu.make_async_copy(part, part, c_s).wait()


def gelu_kernel(v, out_hbm, outv, sem):
    s = lax.axis_index("gy") % 2
    ready = pl.ds(pl.multiple_of(s * 1024, 1024), 1024)
    copies = [pltpu.make_async_copy(v.at[ready], out_hbm.at[ready], sem.at[4])]
    copies[0].start()
    for n in range(4):
        start = pl.multiple_of((1 - s) * 1024 + 256 * n, 256)
        for m in range(4):
            outv[pl.ds(256 * n + 64 * m, 64), :] = gelu(v[pl.ds(start + 64 * m, 64), :])
        copy = pltpu.make_async_copy(outv.at[pl.ds(256 * n, 256)], out_hbm.at[pl.ds(start, 256)], sem.at[n])
        copy.start()
        copies.append(copy)
    for copy in copies:
        copy.wait()


def shards(features, conv_weight, mix_weight):
    f2 = features.reshape(2048, 128)
    f3 = features.reshape(16, 128, 128)
    w = mix_weight.reshape(512, 27)
    cw = conv_weight.transpose(1, 2, 0).reshape(256, 27)
    consts = [jnp.asarray(TABLES[n]) for n in NAMES]
    vm = pltpu.VMEM
    dma = pltpu.SemaphoreType.DMA
    scratch = [
        vm((2048, 128), F32), vm((512, 27), F32), vm((256, 27), F32),
        vm((24, 384), BF16), vm((96, 128), BF16), vm((2, 16, 24, 128), F32), vm((256, 256), BF16), vm((256, 256), BF16),
        vm((256, 128), BF16), vm((2, 256, 128), BF16), vm((3, 8, 128), F32), vm((3, 8, 128), F32), vm((32, 27), F32),
        vm((96, 96), BF16), vm((64, 192), BF16),
        vm((27, 4, 128), F32), vm((2, 24, 4, 128), F32), vm((2, 2, 24, 256), F32), vm((512, 18 * 128), BF16), vm((1152, 512), BF16),
        vm((3, 512, 128), F32),
        vm((2, 128, 128), F32), vm((2, 128, 128), F32), vm((2, 16, 16, 128), F32), vm((4, 16, 128), F32),
        vm((4, 16, 128), F32), vm((2, 192, 128), F32), vm((192, 128), F32), vm((288, 128), F32), vm((3, 72, 128), F32),
        vm((73, 1, 128), F32), vm((64, 2, 1, 128), F32), vm((32, 2, 1, 128), F32), vm((64, 2, 1, 128), F32),
        vm((4, 96, 128), F32), vm((2, 192, 128), F32), vm((192, 128), F32), vm((2048, 128), F32),
        dma((16,)), dma((4,)), dma((4,)), dma((8,)), dma((8,)), dma((3,)), dma((3,)), dma, dma, dma, dma,
        dma((3,)), dma((4,)), dma((27,)), dma((2,)), dma((4,)), dma((4,)),
    ]
    any_spec = pl.BlockSpec(memory_space=pl.ANY)
    vmem_spec = pl.BlockSpec(memory_space=pltpu.VMEM)
    hbm_spec = pl.BlockSpec(memory_space=pltpu.HBM)
    v = pl.pallas_call(
        kernel,
        out_shape=jax.ShapeDtypeStruct((2048, 128), F32),
        in_specs=[hbm_spec] * (4 + len(NAMES)),
        out_specs=vmem_spec,
        scratch_shapes=scratch,
        compiler_params=pltpu.CompilerParams(collective_id=0, has_side_effects=True,
                                             vmem_limit_bytes=40 * 1024 * 1024),
        name="layer",
    )(*[pltpu.with_memory_space_constraint(a, pltpu.HBM) for a in (f2, f3, w, cw, *consts)])
    out = pl.pallas_call(
        gelu_kernel,
        out_shape=jax.ShapeDtypeStruct((2048, 128), F32),
        in_specs=[vmem_spec],
        out_specs=any_spec,
        scratch_shapes=[vm((1024, 128), F32), dma((5,))],
        compiler_params=pltpu.CompilerParams(vmem_limit_bytes=8 * 1024 * 1024),
        name="act",
    )(v)
    return out.reshape(features.shape)


def solution(mesh):
    in_specs = (P(None, "gx", "gy", None), P(), P(None, None, None, "gy", "gx"))
    return jax.shard_map(shards, mesh=mesh, in_specs=in_specs, out_specs=P(None, "gx", "gy", None), check_vma=False)
```
